256 devices in a mesh: ctx: 32 (over y, z), ch: 8 (over x, core).
Axes of the slice: x: 4, y: 4, z: 8, core: 2. Of those that a mesh axis runs over, the one named last changes fastest.
Arguments:
- features: bfloat16 [3, 4096, 4096], P(None, 'ctx', 'ch'), may hold values from -6 to 6
- short_weight: float32 [3, 3, 4096], P(None, None, 'ch'), may hold values from -3 to 3
- filter_taps: bfloat16 [4096, 4096], P('ctx', 'ch'), may hold values from -6 to 6
- decay_rate: float32 [4096], P('ch'), may hold values from 6.1035156e-05 to 0.0007324219
- skip_gain: float32 [4096], P('ch'), may hold values from -1 to 1
- out_weight: bfloat16 [4096, 8192], P('ch'), may hold values from -0.125 to 0.125
Outputs:
- mixed: bfloat16 [4096, 8192], P('ctx', 'ch')
The draws below stay inside these ranges and needn't reach their ends.
All inputs are finite; a program needn't handle non-finite values.
Results may differ from the reference program's by a relative error of at most 0.008.
Values may be sent and summed in bfloat16 or wider, within the bound.
A program may use at most 64 MiB of HBM per device.

```python
import math
import jax
import jax.numpy as jnp

D = 8192
DW = 4096
TAPS = 3
TOKENS = 4096


def strengthened(drawn, stream_key, source, target, shards_of, factor):
    owner, partner = [(jnp.arange(drawn.shape[dim]) // (drawn.shape[dim] // shards_of)).reshape([-1 if axis == dim else 1 for axis in range(drawn.ndim)]) for dim in (source, target)]
    chosen = jax.random.permutation(stream_key, shards_of)[partner]
    strong = (owner == chosen) | (owner == (partner + shards_of // 2) % shards_of)
    return jnp.where(strong, factor * drawn, drawn)


def shard_levels(rng, extent, shards, least, largest):
    factor_of, own = 1.0, jax.random.fold_in(rng, 6)
    for dim, parts in shards:
        heights = jnp.exp(jax.random.uniform(jax.random.fold_in(own, dim), (parts,), jnp.float32, least / len(shards), largest / len(shards)))
        factor_of = factor_of * jnp.repeat(heights, extent[dim] // parts).reshape([-1 if axis == dim else 1 for axis in range(len(extent))])
    return factor_of


def scatter_about(key, extent, spread, most, cuts=(), dtype=jnp.bfloat16):
    result = spread * jax.random.normal(key, extent, jnp.float32)
    if cuts:
        result = result * shard_levels(key, extent, cuts, -0.22, 0.18)
    return jnp.clip(result, -most, most).astype(dtype)


def noise_with(key, shape, spread, bound, shards, heavy, dtype=jnp.bfloat16):
    drawn = spread * jax.random.normal(key, shape, jnp.float32)
    if shards:
        drawn = drawn * shard_levels(key, shape, shards, -0.22, 0.18)
    return jnp.clip(strengthened(drawn, jax.random.fold_in(key, 3), *heavy), -bound, bound).astype(dtype)


def setup_inputs(seed: int = 0) -> dict:
    keys = jax.random.split(jax.random.key(seed), 7)
    return {
        "features": scatter_about(keys[0], (3, TOKENS, DW), 1.0, 6.0, ((1, 32), (2, 8))),
        "short_weight": scatter_about(keys[1], (3, TAPS, DW), 0.6, 3.0, ((2, 8),), jnp.float32),
        "filter_taps": scatter_about(keys[2], (TOKENS, DW), 1.0, 6.0, ((0, 32), (1, 8))),
        "decay_rate": jnp.clip(jnp.exp(math.log(0.0007324219) - 2.4849066 * jax.random.uniform(keys[3], (DW,), jnp.float32) ** shard_levels(keys[3], (DW,), ((0, 8),), -0.2, 0.2)), 6.103515625e-05, 0.0007324219),
        "skip_gain": jnp.clip(jax.random.uniform(keys[4], (DW,), jnp.float32, -1.0, 1.0) * shard_levels(keys[4], (DW,), ((0, 8),), -0.4, 0.0), -1.0, 1.0),
        "out_weight": noise_with(keys[5], (DW, D), DW ** -0.5, 0.125, ((0, 8),), (0, 1, 8, 2.0)),
    }


def reference(features, short_weight, filter_taps, decay_rate, skip_gain, out_weight):
    inputs = features.astype(jnp.float32)
    padded = jnp.pad(inputs, ((0, 0), (2, 0), (0, 0)))
    featured = short_weight[:, 0, None, :] * inputs + short_weight[:, 1, None, :] * padded[:, 1:-1, :] + short_weight[:, 2, None, :] * padded[:, :-2, :]
    product = (featured[1] * featured[2]).astype(jnp.bfloat16)
    positions = jnp.arange(TOKENS).astype(jnp.float32)
    impulse = filter_taps.astype(jnp.float32) * jnp.exp(-decay_rate[None, :] * positions[:, None]) * jnp.sqrt(2.0 * decay_rate)[None, :]
    padded_len = 2 * TOKENS
    spectrum = jnp.fft.rfft(impulse, n=padded_len, axis=0) * jnp.fft.rfft(product.astype(jnp.float32), n=padded_len, axis=0)
    convolved = jnp.fft.irfft(spectrum, n=padded_len, axis=0)[:TOKENS]
    gated = (featured[0] * (convolved + skip_gain[None, :] * product.astype(jnp.float32))).astype(jnp.bfloat16)
    return jnp.dot(gated, out_weight, preferred_element_type=jnp.float32).astype(jnp.bfloat16)
```

```python
import functools

import jax
import jax.numpy as jnp
import numpy as np
from jax import lax
from jax.experimental import pallas as pl
from jax.experimental.pallas import tpu as pltpu
from jax.sharding import PartitionSpec as P

MESH = pl.DeviceIdType.MESH
F32, BF16 = jnp.float32, jnp.bfloat16


def spectral_tables(blocks, length, group):
    total = blocks * length
    coarse = np.arange(blocks)
    fine = np.arange(length)
    stage = np.exp(2j * np.pi * np.outer(coarse + 0.25, coarse) / blocks)
    twist = np.exp(2j * np.pi * np.outer(coarse + 0.25, fine) / total)
    inner = np.exp(2j * np.pi * np.outer(fine, fine) / length)
    wide = np.repeat(np.concatenate([stage.real, stage.imag], 0), group, axis=1)
    tall = np.repeat(np.concatenate([stage.real.T, stage.imag.T], 1), group, axis=1)
    forward = np.block([[inner.real, inner.imag], [-inner.imag, inner.real]])
    back = np.conj(inner).T / total
    inverse = np.block([[back.real, back.imag], [-back.imag, back.real]])
    as_f32 = lambda a: jnp.asarray(np.asarray(a, np.float32))
    return (
        as_f32(wide),
        as_f32(tall),
        as_f32(np.stack([twist.real, twist.imag])),
        as_f32(np.stack([forward, inverse])),
    )


def dot(a, b):
    return jnp.dot(a, b, preferred_element_type=F32)


def halves(value):
    high = value.astype(BF16)
    return high, (value - high.astype(F32)).astype(BF16)


def kernel(
    blocks,
    feat,
    short_w,
    taps,
    decay,
    skip,
    weight,
    wide,
    tall,
    twist,
    inner,
    out,
    featv,
    tapv,
    widev,
    tallv,
    twistv,
    innerv,
    halo,
    tsend,
    trecv,
    psend,
    precv,
    csend,
    crecv,
    gatedv,
    gatedp,
    wown,
    wprt,
    first,
    prodv,
    mhi,
    mlo,
    ihi,
    ilo,
    twc,
    tws,
    dhi,
    dlo,
    hspec,
    spectrum,
    partial,
    kept,
    opp_s,
    plus_s,
    minus_s,
    opp_r,
    plus_r,
    minus_r,
    local_sem,
    send_sem,
    recv_sem,
):
    rows, width = taps.shape
    group = width // blocks
    span = out.shape[1]
    half = span // 2
    c = lax.axis_index("ctx")
    h = lax.axis_index("ch")
    x, core = h // 2, lax.rem(h, 2)
    xs = lax.axis_size("ch") // 2
    partner = x * 2 + 1 - core
    up = lax.rem(x + 1, xs) * 2 + core
    down = lax.rem(x + xs - 1, xs) * 2 + core
    after = lax.rem(c + 1, blocks)

    def local(src, dst, i):
        return pltpu.make_async_copy(src, dst, local_sem.at[i])

    loads = [
        local(taps, tapv, 0),
        local(feat, featv, 1),
        local(wide, widev, 2),
        local(tall, tallv, 3),
        local(twist, twistv, 4),
        local(inner, innerv, 5),
    ]
    for load in loads:
        load.start()

    barrier = pltpu.get_barrier_semaphore()

    def greet(off, carry):
        pl.semaphore_signal(
            barrier, inc=1, device_id={"ctx": lax.rem(c + off, blocks)}, device_id_type=MESH
        )
        return carry

    lax.fori_loop(1, blocks, greet, 0)
    for peer in (partner, up, down):
        pl.semaphore_signal(barrier, inc=1, device_id={"ch": peer}, device_id_type=MESH)

    loads[0].wait()
    places = (c * rows + lax.broadcasted_iota(jnp.int32, (rows, 128), 0)).astype(F32)

    def window(i, carry):
        cols = pl.ds(pl.multiple_of(i * 128, 128), 128)
        rate = decay[:, cols]
        block = tapv[:, cols].astype(F32) * jnp.exp(-rate * places) * jnp.sqrt(2.0 * rate)
        tsend[cols, :] = block.T.astype(BF16)
        return carry

    lax.fori_loop(0, width // 128, window, 0)
    trecv[pl.ds(c * group, group), :] = tsend[pl.ds(c * group, group), :]

    pl.semaphore_wait(barrier, blocks - 1 + 3)

    def remote(src, dst, i, peer):
        return pltpu.make_async_remote_copy(
            src_ref=src,
            dst_ref=dst,
            send_sem=send_sem.at[i],
            recv_sem=recv_sem.at[i],
            device_id=peer,
            device_id_type=MESH,
        )

    edge = remote(feat.at[:, pl.ds(rows - 8, 8), :], halo, 0, {"ctx": after})
    edge.start()

    def spread(src, dst, i):
        mine = dst.at[pl.ds(c * group, group), :]

        def send(off, carry):
            peer = lax.rem(c + off, blocks)
            remote(src.at[pl.ds(peer * group, group), :], mine, i, {"ctx": peer}).start()
            return carry

        lax.fori_loop(1, blocks, send, 0)

    def spread_all(src, dst, i):
        count = (blocks - 1) * group
        return remote(src.at[pl.ds(0, count), :], dst.at[pl.ds(0, count), :], i, {"ctx": after})

    spread(tsend, trecv, 1)

    loads[1].wait()
    edge.wait()
    row = lax.broadcasted_iota(jnp.int32, (rows, 128), 0)

    def featurize(i, carry):
        cols = pl.ds(pl.multiple_of(i * 128, 128), 128)

        def stream(g):
            now = featv[g, :, cols].astype(F32)
            rim = jnp.where(c > 0, halo[g, :, cols].astype(F32), 0.0)
            one = jnp.where(row == 0, rim[7:8], pltpu.roll(now, 1, 0))
            two = pltpu.roll(now, 2, 0)
            two = jnp.where(row == 0, rim[6:7], jnp.where(row == 1, rim[7:8], two))
            w = short_w[g, :, cols]
            return w[0:1] * now + w[1:2] * one + w[2:3] * two

        product = (stream(1) * stream(2)).astype(BF16)
        prodv[:, cols] = product
        psend[cols, :] = product.astype(F32).T.astype(BF16)
        first[:, cols] = stream(0)
        return carry

    lax.fori_loop(0, width // 128, featurize, 0)
    spread(psend, precv, 2)
    precv[pl.ds(c * group, group), :] = psend[pl.ds(c * group, group), :]

    for d in range(xs):
        here = pl.ds(pl.multiple_of((2 * d + core) * span, 128), span)
        there = pl.ds(pl.multiple_of((2 * d + 1 - core) * span, 128), span)
        local(weight.at[:, here], wown.at[:, d * span : (d + 1) * span], 6 + d).start()
        remote(
            weight.at[:, there], wprt.at[:, d * span : (d + 1) * span], 3 + d, {"ch": partner}
        ).start()

    for i in range(2, 6):
        loads[i].wait()
    wide_mask = (
        lax.rem(lax.broadcasted_iota(jnp.int32, (group, width), 1), group)
        == lax.broadcasted_iota(jnp.int32, (group, width), 0)
    )

    def build(j, carry):
        high, low = halves(jnp.where(wide_mask, widev[pl.ds(j, 1), :], 0.0))
        at = pl.ds(pl.multiple_of(j * group, group), group)
        mhi[at, :] = high
        mlo[at, :] = low
        return carry

    lax.fori_loop(0, 2 * blocks, build, 0)
    tall_mask = (
        lax.rem(lax.broadcasted_iota(jnp.int32, (group, 2 * width), 1), group)
        == lax.broadcasted_iota(jnp.int32, (group, 2 * width), 0)
    )

    def build_back(j, carry):
        high, low = halves(jnp.where(tall_mask, tallv[pl.ds(j, 1), :], 0.0))
        at = pl.ds(pl.multiple_of(j * group, group), group)
        ihi[at, :] = high
        ilo[at, :] = low
        twc[at, :] = jnp.broadcast_to(twistv[0, pl.ds(j, 1), :], (group, rows))
        tws[at, :] = jnp.broadcast_to(twistv[1, pl.ds(j, 1), :], (group, rows))
        return carry

    lax.fori_loop(0, blocks, build_back, 0)
    for i in range(2):
        dhi[i], dlo[i] = halves(innerv[i])

    def fine(value, i):
        high, low = halves(value)
        return dot(high, dhi[i]) + (dot(low, dhi[i]) + dot(high, dlo[i]))

    def transformed(data, i):
        at = pl.ds(pl.multiple_of(i * 128, 128), 128)
        lower = pl.ds(pl.multiple_of(width + i * 128, 128), 128)
        real = dot(mhi[at, :], data) + dot(mlo[at, :], data)
        imag = dot(mhi[lower, :], data) + dot(mlo[lower, :], data)
        cosine, sine = twc[at, :], tws[at, :]
        turned = jnp.concatenate(
            [real * cosine - imag * sine, real * sine + imag * cosine], axis=1
        )
        return fine(turned, 0)

    spread_all(tsend, trecv, 1).wait_recv()

    def filter_spectrum(i, carry):
        hspec[pl.ds(pl.multiple_of(i * 128, 128), 128), :] = transformed(trecv[...], i)
        return carry

    lax.fori_loop(0, width // 128, filter_spectrum, 0)

    spread_all(psend, precv, 2).wait_recv()

    def through(i, carry):
        at = pl.ds(pl.multiple_of(i * 128, 128), 128)
        lower = pl.ds(pl.multiple_of(width + i * 128, 128), 128)
        data = transformed(precv[...], i)
        filt = hspec[at, :]
        dr, di, fr, fi = data[:, :rows], data[:, rows:], filt[:, :rows], filt[:, rows:]
        back = fine(jnp.concatenate([dr * fr - di * fi, dr * fi + di * fr], axis=1), 1)
        br, bi = back[:, :rows], back[:, rows:]
        cosine, sine = twc[at, :], tws[at, :]
        spectrum[at, :] = (br * cosine + bi * sine).astype(BF16)
        spectrum[lower, :] = (bi * cosine - br * sine).astype(BF16)
        return carry

    lax.fori_loop(0, width // 128, through, 0)

    def settle(i, carry):
        at = pl.ds(pl.multiple_of(i * 128, 128), 128)
        value = dot(ihi[at, :], spectrum[...]) + dot(ilo[at, :], spectrum[...])
        csend[at, :] = value.astype(BF16)
        return carry

    lax.fori_loop(0, width // 128, settle, 0)
    spread(csend, crecv, 7)
    crecv[pl.ds(c * group, group), :] = csend[pl.ds(c * group, group), :]
    spread_all(csend, crecv, 7).wait_recv()

    def gate(i, carry):
        cols = pl.ds(pl.multiple_of(i * 128, 128), 128)
        convolved = crecv[cols, :].astype(F32).T
        direct = skip[:, cols] * prodv[:, cols].astype(F32)
        gatedv[:, cols] = (first[:, cols] * (convolved + direct)).astype(BF16)
        return carry

    lax.fori_loop(0, width // 128, gate, 0)
    share = remote(gatedv, gatedp, 8, {"ch": partner})
    share.start()

    for d in range(xs):
        local(weight.at[:, pl.ds(0, span)], wown.at[:, d * span : (d + 1) * span], 6 + d).wait()

    def own_part(i, carry):
        cols = pl.ds(pl.multiple_of(i * half, half), half)
        partial[:, cols] = dot(gatedv[...], wown[:, cols])
        return carry

    lax.fori_loop(0, 2 * xs, own_part, 0)
    share.wait_recv()
    for d in range(xs):
        remote(
            weight.at[:, pl.ds(0, span)],
            wprt.at[:, d * span : (d + 1) * span],
            3 + d,
            {"ch": partner},
        ).wait_recv()

    def block(dest, side):
        cols = pl.ds(pl.multiple_of(dest * span + side * half, half), half)
        return partial[:, cols] + dot(gatedp[...], wprt[:, cols])

    far, high, low = lax.rem(x + 2, xs), lax.rem(x + 1, xs), lax.rem(x + xs - 1, xs)
    opp_s[0] = block(far, 0).astype(BF16)
    opp_up = remote(opp_s.at[0], opp_r.at[0], 9, {"ch": up})
    opp_up.start()
    opp_s[1] = block(far, 1).astype(BF16)
    opp_down = remote(opp_s.at[1], opp_r.at[1], 10, {"ch": down})
    opp_down.start()
    plus_s[1] = block(high, 1).astype(BF16)
    plus_one = remote(plus_s.at[1], plus_r.at[1], 11, {"ch": up})
    plus_one.start()
    minus_s[0] = block(low, 0).astype(BF16)
    minus_zero = remote(minus_s.at[0], minus_r.at[0], 12, {"ch": down})
    minus_zero.start()
    kept[0] = block(high, 0)
    kept[1] = block(low, 1)
    opp_up.wait_recv()
    plus_s[0] = (kept[0] + opp_r[0].astype(F32)).astype(BF16)
    plus_zero = remote(plus_s.at[0], plus_r.at[0], 13, {"ch": up})
    plus_zero.start()
    opp_down.wait_recv()
    minus_s[1] = (kept[1] + opp_r[1].astype(F32)).astype(BF16)
    minus_one = remote(minus_s.at[1], minus_r.at[1], 14, {"ch": down})
    minus_one.start()
    own = [block(x, 0), block(x, 1)]
    plus_one.wait_recv()
    minus_zero.wait_recv()
    plus_zero.wait_recv()
    out[:, 0:half] = (own[0] + plus_r[0].astype(F32) + minus_r[0].astype(F32)).astype(BF16)
    minus_one.wait_recv()
    out[:, half:span] = (own[1] + plus_r[1].astype(F32) + minus_r[1].astype(F32)).astype(BF16)

    for i, (src, dst) in ((1, (tsend, trecv)), (2, (psend, precv)), (7, (csend, crecv))):
        spread_all(src, dst, i).wait_send()
    for d in range(xs):
        remote(
            weight.at[:, pl.ds(0, span)],
            wprt.at[:, d * span : (d + 1) * span],
            3 + d,
            {"ch": partner},
        ).wait_send()
    for copy in (share, opp_up, opp_down, plus_one, minus_zero, plus_zero, minus_one):
        copy.wait_send()


def on_device(features, short_weight, filter_taps, decay_rate, skip_gain, out_weight):
    blocks = lax.axis_size("ctx")
    rows, width = filter_taps.shape
    columns = out_weight.shape[1]
    span = columns // lax.axis_size("ch")
    group = width // blocks
    tables = spectral_tables(blocks, rows, group)
    vmem = lambda shape, dtype: pltpu.VMEM(shape, dtype)
    hbm, whole = pl.BlockSpec(memory_space=pl.ANY), pl.BlockSpec(memory_space=pltpu.VMEM)
    import functools

    return pl.pallas_call(
        functools.partial(kernel, blocks),
        out_shape=jax.ShapeDtypeStruct((rows, span), BF16),
        in_specs=[hbm, whole, hbm, whole, whole, hbm, hbm, hbm, hbm, hbm],
        out_specs=whole,
        scratch_shapes=[
            vmem(features.shape, BF16),
            vmem(filter_taps.shape, BF16),
            *[vmem(t.shape, F32) for t in tables],
            vmem((3, 8, width), BF16),
            *[vmem((width, rows), BF16) for _ in range(6)],
            vmem((rows, width), BF16),
            vmem((rows, width), BF16),
            vmem((width, columns // 2), BF16),
            vmem((width, columns // 2), BF16),
            vmem((rows, width), F32),
            vmem((rows, width), BF16),
            vmem((2 * width, width), BF16),
            vmem((2 * width, width), BF16),
            vmem((width, 2 * width), BF16),
            vmem((width, 2 * width), BF16),
            vmem((width, rows), F32),
            vmem((width, rows), F32),
            vmem((2, 2 * rows, 2 * rows), BF16),
            vmem((2, 2 * rows, 2 * rows), BF16),
            vmem((width, 2 * rows), F32),
            vmem((2 * width, rows), BF16),
            vmem((rows, columns // 2), F32),
            vmem((2, rows, span // 2), F32),
            *[vmem((2, rows, span // 2), BF16) for _ in range(6)],
            pltpu.SemaphoreType.DMA((10,)),
            pltpu.SemaphoreType.DMA((15,)),
            pltpu.SemaphoreType.DMA((15,)),
        ],
        compiler_params=pltpu.CompilerParams(
            collective_id=0, has_side_effects=True, vmem_limit_bytes=60 * 1024 * 1024
        ),
    )(
        features,
        short_weight,
        filter_taps,
        decay_rate[None, :],
        skip_gain[None, :],
        out_weight,
        *tables,
    )


def solution(mesh):
    return jax.shard_map(
        on_device,
        mesh=mesh,
        in_specs=(
            P(None, "ctx", "ch"),
            P(None, None, "ch"),
            P("ctx", "ch"),
            P("ch"),
            P("ch"),
            P("ch", None),
        ),
        out_specs=P("ctx", "ch"),
        check_vma=False,
    )
```

```python
import functools

import jax
import jax.numpy as jnp
import numpy as np
from jax import lax
from jax.experimental import pallas as pl
from jax.experimental.pallas import tpu as pltpu
from jax.sharding import PartitionSpec as P

MESH = pl.DeviceIdType.MESH
F32, BF16 = jnp.float32, jnp.bfloat16
DEPTH_Y = 4


def spectral_tables(blocks, length):
    total = blocks * length
    coarse = np.arange(blocks)
    fine = np.arange(length)
    stage = np.exp(2j * np.pi * np.outer(coarse + 0.25, coarse) / blocks)
    twist = np.exp(2j * np.pi * np.outer(coarse + 0.25, fine) / total)
    inner = np.exp(2j * np.pi * np.outer(fine, fine) / length)
    down = np.concatenate([stage.real, stage.imag], 0)
    across = np.concatenate([stage.real.T, stage.imag.T], 1)
    forward = np.block([[inner.real, inner.imag], [-inner.imag, inner.real]])
    back = np.conj(inner).T / total
    inverse = np.block([[back.real, back.imag], [-back.imag, back.real]])

    def parts(value):
        value = np.asarray(value, np.float32)
        high = value.astype(jnp.bfloat16)
        return high, (value - high.astype(np.float32)).astype(jnp.bfloat16)

    return (
        jnp.asarray(np.concatenate(parts(down), 1)),
        jnp.asarray(np.concatenate(parts(across), 1)),
        jnp.asarray(np.stack([twist.real, twist.imag]).astype(np.float32)),
        jnp.asarray(np.stack([*parts(forward), *parts(inverse)])),
    )


def dot(a, b):
    return jnp.dot(a, b, preferred_element_type=F32)


def halves(value):
    high = value.astype(BF16)
    return high, (value - high.astype(F32)).astype(BF16)


def kernel(
    blocks,
    feat,
    short_w,
    taps,
    decay,
    skip,
    weight,
    split,
    join,
    twist,
    inner,
    out,
    featv,
    tapv,
    splitv,
    joinv,
    twistv,
    innerv,
    halo,
    tsend,
    trecv,
    psend,
    precv,
    csend,
    crecv,
    gatedv,
    gatedp,
    wown,
    wprt,
    first,
    prodv,
    staged,
    hspec,
    kept,
    opp_s,
    plus_s,
    minus_s,
    opp_r,
    plus_r,
    minus_r,
    local_sem,
    send_sem,
    recv_sem,
):
    rows, width = taps.shape
    group = width // blocks
    span = out.shape[1]
    half = span // 2
    c = lax.axis_index("ctx")
    h = lax.axis_index("ch")
    x, core = h // 2, lax.rem(h, 2)
    xs = lax.axis_size("ch") // 2
    partner = x * 2 + 1 - core
    up = lax.rem(x + 1, xs) * 2 + core
    down = lax.rem(x + xs - 1, xs) * 2 + core
    after = lax.rem(c + 1, blocks)

    def local(src, dst, i):
        return pltpu.make_async_copy(src, dst, local_sem.at[i])

    loads = [
        local(taps, tapv, 0),
        local(feat, featv, 1),
        local(split, splitv, 2),
        local(join, joinv, 3),
        local(twist, twistv, 4),
        local(inner, innerv, 5),
    ]
    for load in loads:
        load.start()

    barrier = pltpu.get_barrier_semaphore()

    def greet(off, carry):
        pl.semaphore_signal(
            barrier, inc=1, device_id={"ctx": lax.rem(c + off, blocks)}, device_id_type=MESH
        )
        return carry

    lax.fori_loop(1, blocks, greet, 0)
    for peer in (partner, up, down):
        pl.semaphore_signal(barrier, inc=1, device_id={"ch": peer}, device_id_type=MESH)

    loads[0].wait()
    places = (c * rows + lax.broadcasted_iota(jnp.int32, (rows, 128), 0)).astype(F32)

    def window(i, carry):
        cols = pl.ds(pl.multiple_of(i * 128, 128), 128)
        rate = decay[:, cols]
        block = tapv[:, cols].astype(F32) * jnp.exp(-rate * places) * jnp.sqrt(2.0 * rate)
        tsend[cols, :] = block.T.astype(BF16)
        return carry

    lax.fori_loop(0, width // 128, window, 0)
    trecv[pl.ds(c * group, group), :] = tsend[pl.ds(c * group, group), :]

    pl.semaphore_wait(barrier, blocks - 1 + 3)

    def remote(src, dst, i, peer):
        return pltpu.make_async_remote_copy(
            src_ref=src,
            dst_ref=dst,
            send_sem=send_sem.at[i],
            recv_sem=recv_sem.at[i],
            device_id=peer,
            device_id_type=MESH,
        )

    edge = remote(feat.at[:, pl.ds(rows - 8, 8), :], halo, 0, {"ctx": after})
    edge.start()

    def zigzag(i, size):
        return size // 2 + lax.rem(i + 1, 2) * (i // 2) - lax.rem(i, 2) * ((i + 1) // 2)

    def toward(i, j):
        depth_z = blocks // DEPTH_Y
        y = lax.rem(c // depth_z + zigzag(i, DEPTH_Y), DEPTH_Y)
        z = lax.rem(c + zigzag(j, depth_z), depth_z)
        return y * depth_z + z

    depth_z = blocks // DEPTH_Y
    my_y, my_z = c // depth_z, lax.rem(c, depth_z)

    def spread(src, dst, i):
        mine = dst.at[pl.ds(c * group, group), :]

        def send(step, z):
            peer = lax.rem(my_y + 2 + step, DEPTH_Y) * depth_z + z
            remote(src.at[pl.ds(peer * group, group), :], mine, i, {"ctx": peer}).start()
            return z

        for far in (4, 3, 5, 2, 6, 1, 7):
            lax.fori_loop(0, DEPTH_Y, send, lax.rem(my_z + far, depth_z))
        for step in (0, 1, 3):
            send(step, my_z)

    def spread_all(src, dst, i):
        count = (blocks - 1) * group
        return remote(src.at[pl.ds(0, count), :], dst.at[pl.ds(0, count), :], i, {"ctx": after})

    spread(tsend, trecv, 1)

    loads[1].wait()
    edge.wait()
    row = lax.broadcasted_iota(jnp.int32, (rows, 128), 0)

    def featurize(i, carry):
        cols = pl.ds(pl.multiple_of(i * 128, 128), 128)

        def stream(g):
            now = featv[g, :, cols].astype(F32)
            rim = jnp.where(c > 0, halo[g, :, cols].astype(F32), 0.0)
            one = jnp.where(row == 0, rim[7:8], pltpu.roll(now, 1, 0))
            two = pltpu.roll(now, 2, 0)
            two = jnp.where(row == 0, rim[6:7], jnp.where(row == 1, rim[7:8], two))
            w = short_w[g, :, cols]
            return w[0:1] * now + w[1:2] * one + w[2:3] * two

        product = (stream(1) * stream(2)).astype(BF16)
        prodv[:, cols] = product
        psend[cols, :] = product.astype(F32).T.astype(BF16)
        first[:, cols] = stream(0)
        return carry

    lax.fori_loop(0, width // 128, featurize, 0)
    spread(psend, precv, 2)
    precv[pl.ds(c * group, group), :] = psend[pl.ds(c * group, group), :]

    for d in range(xs):
        here = pl.ds(pl.multiple_of((2 * d + core) * span, 128), span)
        there = pl.ds(pl.multiple_of((2 * d + 1 - core) * span, 128), span)
        local(weight.at[:, here], wown.at[:, d * span : (d + 1) * span], 6 + d).start()
        remote(
            weight.at[:, there], wprt.at[:, d * span : (d + 1) * span], 3 + d, {"ch": partner}
        ).start()

    for i in range(2, 6):
        loads[i].wait()
    cosine, sine = twistv[0], twistv[1]
    lump = 8
    tall = lump * blocks

    def fine(value, i):
        high, low = halves(value)
        return dot(high, innerv[2 * i]) + (dot(low, innerv[2 * i]) + dot(high, innerv[2 * i + 1]))

    def lanes(q):
        return slice(q * rows, (q + 1) * rows)

    def tile(q):
        return slice(q * blocks, (q + 1) * blocks)

    def transformed(first_channel):
        data = jnp.concatenate(
            [staged[pl.ds(first_channel + q, blocks, stride=group), :] for q in range(lump)], axis=1
        ).astype(BF16)
        coarse = dot(splitv[...], jnp.concatenate([data, data], axis=0))
        real, imag = coarse[:blocks], coarse[blocks:]
        turned = []
        for q in range(lump):
            r, i = real[:, lanes(q)], imag[:, lanes(q)]
            turned.append(
                jnp.concatenate([r * cosine - i * sine, r * sine + i * cosine], axis=1)
            )
        return fine(jnp.concatenate(turned, axis=0), 0)

    spread_all(tsend, trecv, 1).wait_recv()
    staged[...] = trecv[...].astype(F32)

    def filter_spectrum(n, carry):
        hspec[pl.ds(pl.multiple_of(n * tall, tall), tall), :] = transformed(n * lump)
        return carry

    lax.fori_loop(0, group // lump, filter_spectrum, 0)

    spread_all(psend, precv, 2).wait_recv()
    staged[...] = precv[...].astype(F32)

    def through(n, carry):
        data = transformed(n * lump)
        filt = hspec[pl.ds(pl.multiple_of(n * tall, tall), tall), :]
        dr, di, fr, fi = data[:, :rows], data[:, rows:], filt[:, :rows], filt[:, rows:]
        back = fine(jnp.concatenate([dr * fr - di * fi, dr * fi + di * fr], axis=1), 1)
        turned = []
        for q in range(lump):
            r, i = back[tile(q), :rows], back[tile(q), rows:]
            turned.append(jnp.concatenate([r * cosine + i * sine, i * cosine - r * sine], axis=0))
        spectrum = jnp.concatenate(turned, axis=1).astype(BF16)
        value = dot(joinv[...], jnp.concatenate([spectrum, spectrum], axis=0))
        for q in range(lump):
            staged[pl.ds(n * lump + q, blocks, stride=group), :] = value[:, lanes(q)]
        return carry

    lax.fori_loop(0, group // lump, through, 0)
    csend[...] = staged[...].astype(BF16)
    spread(csend, crecv, 7)
    crecv[pl.ds(c * group, group), :] = csend[pl.ds(c * group, group), :]
    spread_all(csend, crecv, 7).wait_recv()

    def gate(i, carry):
        cols = pl.ds(pl.multiple_of(i * 128, 128), 128)
        convolved = crecv[cols, :].astype(F32).T
        direct = skip[:, cols] * prodv[:, cols].astype(F32)
        gatedv[:, cols] = (first[:, cols] * (convolved + direct)).astype(BF16)
        return carry

    lax.fori_loop(0, width // 128, gate, 0)
    share = remote(gatedv, gatedp, 8, {"ch": partner})
    share.start()

    for d in range(xs):
        local(weight.at[:, pl.ds(0, span)], wown.at[:, d * span : (d + 1) * span], 6 + d).wait()

    far, high, low = lax.rem(x + 2, xs), lax.rem(x + 1, xs), lax.rem(x + xs - 1, xs)

    def at_side(dest, side):
        return pl.ds(pl.multiple_of(dest * span + side * half, half), half)

    for side in range(2):
        kept[side] = dot(gatedv[...], wown[:, at_side(far, side)])
    for d in range(xs):
        remote(
            weight.at[:, pl.ds(0, span)],
            wprt.at[:, d * span : (d + 1) * span],
            3 + d,
            {"ch": partner},
        ).wait_recv()

    def block(dest, side):
        cols = at_side(dest, side)
        return dot(gatedv[...], wown[:, cols]) + dot(gatedp[...], wprt[:, cols])

    share.wait_recv()
    opp_s[0] = (kept[0] + dot(gatedp[...], wprt[:, at_side(far, 0)])).astype(BF16)
    opp_up = remote(opp_s.at[0], opp_r.at[0], 9, {"ch": up})
    opp_up.start()
    opp_s[1] = (kept[1] + dot(gatedp[...], wprt[:, at_side(far, 1)])).astype(BF16)
    opp_down = remote(opp_s.at[1], opp_r.at[1], 10, {"ch": down})
    opp_down.start()
    plus_s[1] = block(high, 1).astype(BF16)
    plus_one = remote(plus_s.at[1], plus_r.at[1], 11, {"ch": up})
    plus_one.start()
    minus_s[0] = block(low, 0).astype(BF16)
    minus_zero = remote(minus_s.at[0], minus_r.at[0], 12, {"ch": down})
    minus_zero.start()
    kept[0] = block(high, 0)
    kept[1] = block(low, 1)
    opp_up.wait_recv()
    plus_s[0] = (kept[0] + opp_r[0].astype(F32)).astype(BF16)
    plus_zero = remote(plus_s.at[0], plus_r.at[0], 13, {"ch": up})
    plus_zero.start()
    opp_down.wait_recv()
    minus_s[1] = (kept[1] + opp_r[1].astype(F32)).astype(BF16)
    minus_one = remote(minus_s.at[1], minus_r.at[1], 14, {"ch": down})
    minus_one.start()
    own = [block(x, 0), block(x, 1)]
    plus_one.wait_recv()
    minus_zero.wait_recv()
    plus_zero.wait_recv()
    out[:, 0:half] = (own[0] + plus_r[0].astype(F32) + minus_r[0].astype(F32)).astype(BF16)
    minus_one.wait_recv()
    out[:, half:span] = (own[1] + plus_r[1].astype(F32) + minus_r[1].astype(F32)).astype(BF16)

    for i, (src, dst) in ((1, (tsend, trecv)), (2, (psend, precv)), (7, (csend, crecv))):
        spread_all(src, dst, i).wait_send()
    for d in range(xs):
        remote(
            weight.at[:, pl.ds(0, span)],
            wprt.at[:, d * span : (d + 1) * span],
            3 + d,
            {"ch": partner},
        ).wait_send()
    for copy in (share, opp_up, opp_down, plus_one, minus_zero, plus_zero, minus_one):
        copy.wait_send()


def on_device(features, short_weight, filter_taps, decay_rate, skip_gain, out_weight):
    blocks = lax.axis_size("ctx")
    rows, width = filter_taps.shape
    columns = out_weight.shape[1]
    span = columns // lax.axis_size("ch")
    group = width // blocks
    tables = spectral_tables(blocks, rows)
    vmem = lambda shape, dtype: pltpu.VMEM(shape, dtype)
    hbm, whole = pl.BlockSpec(memory_space=pl.ANY), pl.BlockSpec(memory_space=pltpu.VMEM)

    return pl.pallas_call(
        functools.partial(kernel, blocks),
        out_shape=jax.ShapeDtypeStruct((rows, span), BF16),
        in_specs=[hbm, whole, hbm, whole, whole, hbm, hbm, hbm, hbm, hbm],
        out_specs=whole,
        scratch_shapes=[
            vmem(features.shape, BF16),
            vmem(filter_taps.shape, BF16),
            *[vmem(t.shape, t.dtype) for t in tables],
            vmem((3, 8, width), BF16),
            *[vmem((width, rows), BF16) for _ in range(6)],
            vmem((rows, width), BF16),
            vmem((rows, width), BF16),
            vmem((width, columns // 2), BF16),
            vmem((width, columns // 2), BF16),
            vmem((rows, width), F32),
            vmem((rows, width), BF16),
            vmem((width, rows), F32),
            vmem((width, 2 * rows), F32),
            vmem((2, rows, span // 2), F32),
            *[vmem((2, rows, span // 2), BF16) for _ in range(6)],
            pltpu.SemaphoreType.DMA((10,)),
            pltpu.SemaphoreType.DMA((15,)),
            pltpu.SemaphoreType.DMA((15,)),
        ],
        compiler_params=pltpu.CompilerParams(
            collective_id=0, has_side_effects=True, vmem_limit_bytes=60 * 1024 * 1024
        ),
    )(
        features,
        short_weight,
        filter_taps,
        decay_rate[None, :],
        skip_gain[None, :],
        out_weight,
        *tables,
    )


def solution(mesh):
    return jax.shard_map(
        on_device,
        mesh=mesh,
        in_specs=(
            P(None, "ctx", "ch"),
            P(None, None, "ch"),
            P("ctx", "ch"),
            P("ch"),
            P("ch"),
            P("ch", None),
        ),
        out_specs=P("ctx", "ch"),
        check_vma=False,
    )
```

```python
import functools

import jax
import jax.numpy as jnp
import numpy as np
from jax import lax
from jax.experimental import pallas as pl
from jax.experimental.pallas import tpu as pltpu
from jax.sharding import PartitionSpec as P

MESH = pl.DeviceIdType.MESH
F32, BF16 = jnp.float32, jnp.bfloat16
DEPTH_Y = 4


def spectral_tables(blocks, length):
    total = blocks * length
    coarse = np.arange(blocks)
    fine = np.arange(length)
    stage = np.exp(2j * np.pi * np.outer(coarse + 0.25, coarse) / blocks)
    twist = np.exp(2j * np.pi * np.outer(coarse + 0.25, fine) / total)
    inner = np.exp(2j * np.pi * np.outer(fine, fine) / length)
    down = np.concatenate([stage.real, stage.imag], 0)
    across = np.concatenate([stage.real.T, stage.imag.T], 1)
    forward = np.block([[inner.real, inner.imag], [-inner.imag, inner.real]])
    back = np.conj(inner).T / total
    inverse = np.block([[back.real, back.imag], [-back.imag, back.real]])

    def parts(value):
        value = np.asarray(value, np.float32)
        high = value.astype(jnp.bfloat16)
        return high, (value - high.astype(np.float32)).astype(jnp.bfloat16)

    return (
        jnp.asarray(np.concatenate(parts(down), 1)),
        jnp.asarray(np.concatenate(parts(across), 1)),
        jnp.asarray(np.stack([twist.real, twist.imag]).astype(np.float32)),
        jnp.asarray(np.stack([*parts(forward), *parts(inverse)])),
    )


def dot(a, b):
    return jnp.dot(a, b, preferred_element_type=F32)


def halves(value):
    high = value.astype(BF16)
    return high, (value - high.astype(F32)).astype(BF16)


def kernel(
    blocks,
    feat,
    short_in,
    taps,
    decay_in,
    skip_in,
    weight,
    split,
    join,
    twist,
    inner,
    out,
    featv,
    tapv,
    short_w,
    decay,
    skip,
    splitv,
    joinv,
    twistv,
    innerv,
    halo,
    esend,
    erecv,
    tsend,
    trecv,
    psend,
    precv,
    csend,
    crecv,
    gatedv,
    gatedp,
    wown,
    wprt,
    first,
    prodv,
    staged,
    spec,
    kept,
    opp_s,
    plus_s,
    minus_s,
    opp_r,
    plus_r,
    minus_r,
    local_sem,
    send_sem,
    recv_sem,
):
    rows, width = taps.shape
    group = width // blocks
    span = out.shape[1]
    half = span // 2
    c = lax.axis_index("ctx")
    h = lax.axis_index("ch")
    x, core = h // 2, lax.rem(h, 2)
    xs = lax.axis_size("ch") // 2
    partner = x * 2 + 1 - core
    up = lax.rem(x + 1, xs) * 2 + core
    down = lax.rem(x + xs - 1, xs) * 2 + core
    after = lax.rem(c + 1, blocks)

    def local(src, dst, i):
        return pltpu.make_async_copy(src, dst, local_sem.at[i])

    loads = [
        local(taps, tapv, 0),
        local(feat, featv, 1),
        local(split, splitv, 2),
        local(join, joinv, 3),
        local(twist, twistv, 4),
        local(inner, innerv, 5),
        local(decay_in, decay, 10),
        local(short_in, short_w, 11),
        local(skip_in, skip, 12),
    ]
    for load in loads:
        load.start()

    barrier = pltpu.get_barrier_semaphore()

    def greet(off, carry):
        pl.semaphore_signal(
            barrier, inc=1, device_id={"ctx": lax.rem(c + off, blocks)}, device_id_type=MESH
        )
        return carry

    lax.fori_loop(1, blocks, greet, 0)
    for peer in (partner, up, down):
        pl.semaphore_signal(barrier, inc=1, device_id={"ch": peer}, device_id_type=MESH)

    loads[0].wait()
    loads[6].wait()
    places = (c * rows + lax.broadcasted_iota(jnp.int32, (rows, 128), 0)).astype(F32)

    def window(i, carry):
        cols = pl.ds(pl.multiple_of(i * 128, 128), 128)
        rate = decay[:, cols]
        block = tapv[:, cols].astype(F32) * jnp.exp(-rate * places) * jnp.sqrt(2.0 * rate)
        tsend[cols, :] = block.T.astype(BF16)
        return carry

    lax.fori_loop(0, width // 128, window, 0)
    trecv[pl.ds(c * group, group), :] = tsend[pl.ds(c * group, group), :]

    for i in (1, 7, 8):
        loads[i].wait()
    row = lax.broadcasted_iota(jnp.int32, (rows, 128), 0)
    lane = lax.broadcasted_iota(jnp.int32, (rows, 128), 1)
    eight = lax.broadcasted_iota(jnp.int32, (8, 128), 0)
    per_kind = jnp.where(lax.shift_right_logical(lane, 4) == row, 1.0, 0.0).astype(BF16)
    same_channel = lax.rem(lane, group) == lax.rem(row, group)
    per_peer = jnp.where(
        lax.shift_right_logical(lax.broadcasted_iota(jnp.int32, (8, 128), 1), 4) == eight, 1.0, 0.0
    ).astype(BF16)

    def blend(g, cols, rim):
        now = featv[g, :, cols].astype(F32)
        one = jnp.where(row == 0, rim[7:8], pltpu.roll(now, 1, 0))
        two = pltpu.roll(now, 2, 0)
        two = jnp.where(row == 0, rim[6:7], jnp.where(row == 1, rim[7:8], two))
        w = short_w[g, :, cols]
        return w[0:1] * now + w[1:2] * one + w[2:3] * two

    def early(i, carry):
        cols = pl.ds(pl.multiple_of(i * 128, 128), 128)
        nothing = jnp.zeros((8, 128), F32)
        product = blend(1, cols, nothing) * blend(2, cols, nothing)
        psend[cols, :] = product.T.astype(BF16)
        edges = nothing
        for n, g in enumerate((1, 2)):
            head = featv[g, 0:8, cols].astype(F32)
            tail = featv[g, rows - 8 : rows, cols].astype(F32)
            w = short_w[g, :, cols]
            kinds = (
                (2 * n, w[0:1] * head[0:1]),
                (2 * n + 1, w[0:1] * head[1:2] + w[1:2] * head[0:1]),
                (2 * n + 4, w[1:2] * tail[7:8] + w[2:3] * tail[6:7]),
                (2 * n + 5, w[2:3] * tail[7:8]),
            )
            for at, value in kinds:
                edges = jnp.where(eight == at, value, edges)
        turned = jnp.concatenate([edges, jnp.zeros((rows - 8, 128), F32)], axis=0).T
        high, low = halves(turned)
        wide = jnp.where(same_channel, dot(high, per_kind) + dot(low, per_kind), 0.0)
        high, low = halves(wide)
        esend[pl.ds(pl.multiple_of(i * 8, 8), 8), :] = dot(per_peer, high) + dot(per_peer, low)
        return carry

    lax.fori_loop(0, width // 128, early, 0)
    precv[pl.ds(c * group, group), :] = psend[pl.ds(c * group, group), :]
    erecv[pl.ds(c, 1), :] = esend[pl.ds(c, 1), :]

    pl.semaphore_wait(barrier, blocks - 1 + 3)

    def remote(src, dst, i, peer):
        return pltpu.make_async_remote_copy(
            src_ref=src,
            dst_ref=dst,
            send_sem=send_sem.at[i],
            recv_sem=recv_sem.at[i],
            device_id=peer,
            device_id_type=MESH,
        )

    edge = remote(feat.at[:, pl.ds(rows - 8, 8), :], halo, 0, {"ctx": after})
    edge.start()

    def zigzag(i, size):
        return size // 2 + lax.rem(i + 1, 2) * (i // 2) - lax.rem(i, 2) * ((i + 1) // 2)

    def toward(i, j):
        depth_z = blocks // DEPTH_Y
        y = lax.rem(c // depth_z + zigzag(i, DEPTH_Y), DEPTH_Y)
        z = lax.rem(c + zigzag(j, depth_z), depth_z)
        return y * depth_z + z

    depth_z = blocks // DEPTH_Y
    my_y, my_z = c // depth_z, lax.rem(c, depth_z)

    def spread(streams):
        def send(step, z):
            peer = lax.rem(my_y + 2 + step, DEPTH_Y) * depth_z + z
            for src, dst, tall, i in streams:
                remote(
                    src.at[pl.ds(peer * tall, tall), :],
                    dst.at[pl.ds(c * tall, tall), :],
                    i,
                    {"ctx": peer},
                ).start()
            return z

        for far in (4, 3, 5, 2, 6, 1, 7):
            lax.fori_loop(0, DEPTH_Y, send, lax.rem(my_z + far, depth_z))
        for step in (0, 1, 3):
            send(step, my_z)

    def spread_all(src, dst, tall, i):
        count = (blocks - 1) * tall
        return remote(src.at[pl.ds(0, count), :], dst.at[pl.ds(0, count), :], i, {"ctx": after})

    products = (psend, precv, group, 2)
    rims = (esend, erecv, 1, 15)
    filters = (tsend, trecv, group, 1)
    outcomes = (csend, crecv, group, 7)
    spread((rims, products))
    spread((filters,))

    for d in range(xs):
        here = pl.ds(pl.multiple_of((2 * d + core) * span, 128), span)
        there = pl.ds(pl.multiple_of((2 * d + 1 - core) * span, 128), span)
        local(weight.at[:, here], wown.at[:, d * span : (d + 1) * span], 6 + d).start()
        remote(
            weight.at[:, there], wprt.at[:, d * span : (d + 1) * span], 3 + d, {"ch": partner}
        ).start()

    edge.wait()

    def featurize(i, carry):
        cols = pl.ds(pl.multiple_of(i * 128, 128), 128)

        def stream(g):
            return blend(g, cols, jnp.where(c > 0, halo[g, :, cols].astype(F32), 0.0))

        prodv[:, cols] = (stream(1) * stream(2)).astype(BF16)
        first[:, cols] = stream(0)
        return carry

    lax.fori_loop(0, width // 128, featurize, 0)
    for i in range(2, 6):
        loads[i].wait()
    cosine, sine = twistv[0], twistv[1]
    lump = 8
    tall = lump * blocks

    def fine(value, i):
        high, low = halves(value)
        return dot(high, innerv[2 * i]) + (dot(low, innerv[2 * i]) + dot(high, innerv[2 * i + 1]))

    def lanes(q):
        return slice(q * rows, (q + 1) * rows)

    def tile(q):
        return slice(q * blocks, (q + 1) * blocks)

    def transformed(first_channel):
        data = jnp.concatenate(
            [staged[pl.ds(first_channel + q, blocks, stride=group), :] for q in range(lump)], axis=1
        ).astype(BF16)
        coarse = dot(splitv[...], jnp.concatenate([data, data], axis=0))
        real, imag = coarse[:blocks], coarse[blocks:]
        turned = []
        for q in range(lump):
            r, i = real[:, lanes(q)], imag[:, lanes(q)]
            turned.append(
                jnp.concatenate([r * cosine - i * sine, r * sine + i * cosine], axis=1)
            )
        return fine(jnp.concatenate(turned, axis=0), 0)

    spread_all(*rims).wait_recv()
    spread_all(*products).wait_recv()
    staged[...] = precv[...].astype(F32)
    block_row = lax.broadcasted_iota(jnp.int32, (blocks, 128), 0)
    block_lane = lax.broadcasted_iota(jnp.int32, (blocks, 128), 1)
    rim = erecv[...]
    before = jnp.where(block_row == 0, 0.0, pltpu.roll(rim, 1, 0))
    rim = rim + pltpu.roll(before, 64, 1)
    rim = (rim * pltpu.roll(rim, 96, 1)).astype(BF16).astype(F32)
    for q in range(group):
        at = pl.ds(q, blocks, stride=group)
        zero = pltpu.roll(rim, (128 - q) % 128, 1)
        one = pltpu.roll(rim, 113 - q, 1)
        staged[at, :] = jnp.where(
            block_lane == 0, zero, jnp.where(block_lane == 1, one, staged[at, :])
        )

    def product_spectrum(n, carry):
        spec[pl.ds(pl.multiple_of(n * tall, tall), tall), :] = transformed(n * lump)
        return carry

    lax.fori_loop(0, group // lump, product_spectrum, 0)

    spread_all(*filters).wait_recv()
    staged[...] = trecv[...].astype(F32)

    def through(n, carry):
        data = transformed(n * lump)
        filt = spec[pl.ds(pl.multiple_of(n * tall, tall), tall), :]
        dr, di, fr, fi = data[:, :rows], data[:, rows:], filt[:, :rows], filt[:, rows:]
        back = fine(jnp.concatenate([dr * fr - di * fi, dr * fi + di * fr], axis=1), 1)
        turned = []
        for q in range(lump):
            r, i = back[tile(q), :rows], back[tile(q), rows:]
            turned.append(jnp.concatenate([r * cosine + i * sine, i * cosine - r * sine], axis=0))
        spectrum = jnp.concatenate(turned, axis=1).astype(BF16)
        value = dot(joinv[...], jnp.concatenate([spectrum, spectrum], axis=0))
        for q in range(lump):
            staged[pl.ds(n * lump + q, blocks, stride=group), :] = value[:, lanes(q)]
        return carry

    lax.fori_loop(0, group // lump, through, 0)
    csend[...] = staged[...].astype(BF16)
    spread((outcomes,))
    crecv[pl.ds(c * group, group), :] = csend[pl.ds(c * group, group), :]
    spread_all(*outcomes).wait_recv()

    def gate(i, carry):
        cols = pl.ds(pl.multiple_of(i * 128, 128), 128)
        convolved = crecv[cols, :].astype(F32).T
        direct = skip[:, cols] * prodv[:, cols].astype(F32)
        gatedv[:, cols] = (first[:, cols] * (convolved + direct)).astype(BF16)
        return carry

    lax.fori_loop(0, width // 128, gate, 0)
    share = remote(gatedv, gatedp, 8, {"ch": partner})
    share.start()

    for d in range(xs):
        local(weight.at[:, pl.ds(0, span)], wown.at[:, d * span : (d + 1) * span], 6 + d).wait()

    far, high, low = lax.rem(x + 2, xs), lax.rem(x + 1, xs), lax.rem(x + xs - 1, xs)

    def at_side(dest, side):
        return pl.ds(pl.multiple_of(dest * span + side * half, half), half)

    for side in range(2):
        kept[side] = dot(gatedv[...], wown[:, at_side(far, side)])
    for d in range(xs):
        remote(
            weight.at[:, pl.ds(0, span)],
            wprt.at[:, d * span : (d + 1) * span],
            3 + d,
            {"ch": partner},
        ).wait_recv()

    def block(dest, side):
        cols = at_side(dest, side)
        return dot(gatedv[...], wown[:, cols]) + dot(gatedp[...], wprt[:, cols])

    share.wait_recv()
    opp_s[0] = (kept[0] + dot(gatedp[...], wprt[:, at_side(far, 0)])).astype(BF16)
    opp_up = remote(opp_s.at[0], opp_r.at[0], 9, {"ch": up})
    opp_up.start()
    opp_s[1] = (kept[1] + dot(gatedp[...], wprt[:, at_side(far, 1)])).astype(BF16)
    opp_down = remote(opp_s.at[1], opp_r.at[1], 10, {"ch": down})
    opp_down.start()
    plus_s[1] = block(high, 1).astype(BF16)
    plus_one = remote(plus_s.at[1], plus_r.at[1], 11, {"ch": up})
    plus_one.start()
    minus_s[0] = block(low, 0).astype(BF16)
    minus_zero = remote(minus_s.at[0], minus_r.at[0], 12, {"ch": down})
    minus_zero.start()
    kept[0] = block(high, 0)
    kept[1] = block(low, 1)
    opp_up.wait_recv()
    plus_s[0] = (kept[0] + opp_r[0].astype(F32)).astype(BF16)
    plus_zero = remote(plus_s.at[0], plus_r.at[0], 13, {"ch": up})
    plus_zero.start()
    opp_down.wait_recv()
    minus_s[1] = (kept[1] + opp_r[1].astype(F32)).astype(BF16)
    minus_one = remote(minus_s.at[1], minus_r.at[1], 14, {"ch": down})
    minus_one.start()
    own = [block(x, 0), block(x, 1)]
    plus_one.wait_recv()
    minus_zero.wait_recv()
    plus_zero.wait_recv()
    out[:, 0:half] = (own[0] + plus_r[0].astype(F32) + minus_r[0].astype(F32)).astype(BF16)
    minus_one.wait_recv()
    out[:, half:span] = (own[1] + plus_r[1].astype(F32) + minus_r[1].astype(F32)).astype(BF16)

    for stream in (rims, products, filters, outcomes):
        spread_all(*stream).wait_send()
    for d in range(xs):
        remote(
            weight.at[:, pl.ds(0, span)],
            wprt.at[:, d * span : (d + 1) * span],
            3 + d,
            {"ch": partner},
        ).wait_send()
    for copy in (share, opp_up, opp_down, plus_one, minus_zero, plus_zero, minus_one):
        copy.wait_send()


def on_device(features, short_weight, filter_taps, decay_rate, skip_gain, out_weight):
    blocks = lax.axis_size("ctx")
    rows, width = filter_taps.shape
    columns = out_weight.shape[1]
    span = columns // lax.axis_size("ch")
    group = width // blocks
    tables = spectral_tables(blocks, rows)
    stay = lambda value: pltpu.with_memory_space_constraint(value, pltpu.HBM)
    vmem = lambda shape, dtype: pltpu.VMEM(shape, dtype)
    hbm, whole = pl.BlockSpec(memory_space=pltpu.HBM), pl.BlockSpec(memory_space=pltpu.VMEM)

    return pl.pallas_call(
        functools.partial(kernel, blocks),
        out_shape=jax.ShapeDtypeStruct((rows, span), BF16),
        in_specs=[hbm] * 10,
        out_specs=whole,
        scratch_shapes=[
            vmem(features.shape, BF16),
            vmem(filter_taps.shape, BF16),
            vmem(short_weight.shape, F32),
            vmem((1, width), F32),
            vmem((1, width), F32),
            *[vmem(t.shape, t.dtype) for t in tables],
            vmem((3, 8, width), BF16),
            vmem((blocks, 128), F32),
            vmem((blocks, 128), F32),
            *[vmem((width, rows), BF16) for _ in range(6)],
            vmem((rows, width), BF16),
            vmem((rows, width), BF16),
            vmem((width, columns // 2), BF16),
            vmem((width, columns // 2), BF16),
            vmem((rows, width), F32),
            vmem((rows, width), BF16),
            vmem((width, rows), F32),
            vmem((width, 2 * rows), F32),
            vmem((2, rows, span // 2), F32),
            *[vmem((2, rows, span // 2), BF16) for _ in range(6)],
            pltpu.SemaphoreType.DMA((13,)),
            pltpu.SemaphoreType.DMA((16,)),
            pltpu.SemaphoreType.DMA((16,)),
        ],
        compiler_params=pltpu.CompilerParams(
            collective_id=0, has_side_effects=True, vmem_limit_bytes=40000000
        ),
    )(
        stay(features),
        stay(short_weight),
        stay(filter_taps),
        stay(decay_rate[None, :]),
        stay(skip_gain[None, :]),
        stay(out_weight),
        *map(stay, tables),
    )


def solution(mesh):
    return jax.shard_map(
        on_device,
        mesh=mesh,
        in_specs=(
            P(None, "ctx", "ch"),
            P(None, None, "ch"),
            P("ctx", "ch"),
            P("ch"),
            P("ch"),
            P("ch", None),
        ),
        out_specs=P("ctx", "ch"),
        check_vma=False,
    )
```

```python
import functools

import jax
import jax.numpy as jnp
import numpy as np
from jax import lax
from jax.experimental import pallas as pl
from jax.experimental.pallas import tpu as pltpu
from jax.sharding import PartitionSpec as P

MESH = pl.DeviceIdType.MESH
F32, BF16 = jnp.float32, jnp.bfloat16
DEPTH_Y = 4


def spectral_tables(blocks, length):
    total = blocks * length
    coarse = np.arange(blocks)
    fine = np.arange(length)
    stage = np.exp(2j * np.pi * np.outer(coarse + 0.25, coarse) / blocks)
    twist = np.exp(2j * np.pi * np.outer(coarse + 0.25, fine) / total)
    inner = np.exp(2j * np.pi * np.outer(fine, fine) / length)
    down = np.concatenate([stage.real, stage.imag], 0)
    across = np.concatenate([stage.real.T, stage.imag.T], 1)
    forward = np.block([[inner.real, inner.imag], [-inner.imag, inner.real]])
    back = np.conj(inner).T / total
    inverse = np.block([[back.real, back.imag], [-back.imag, back.real]])

    def parts(value):
        value = np.asarray(value, np.float32)
        high = value.astype(jnp.bfloat16)
        return high, (value - high.astype(np.float32)).astype(jnp.bfloat16)

    return (
        jnp.asarray(np.concatenate(parts(down), 1)),
        jnp.asarray(np.concatenate(parts(across), 1)),
        jnp.asarray(np.stack([twist.real, twist.imag]).astype(np.float32)),
        jnp.asarray(np.stack([parts(forward)[0], parts(inverse)[0]])),
    )


def dot(a, b):
    return jnp.dot(a, b, preferred_element_type=F32)


def halves(value):
    high = value.astype(BF16)
    return high, (value - high.astype(F32)).astype(BF16)


def kernel(
    blocks,
    feat,
    short_in,
    taps,
    decay_in,
    skip_in,
    weight,
    split,
    join,
    twist,
    inner,
    out,
    featv,
    tapv,
    short_w,
    decay,
    skip,
    splitv,
    joinv,
    twistv,
    innerv,
    halo,
    esend,
    erecv,
    tsend,
    trecv,
    psend,
    precv,
    csend,
    crecv,
    gatedv,
    gatedp,
    wown,
    wprt,
    first,
    prodv,
    staged,
    spec,
    kept,
    opp_s,
    plus_s,
    minus_s,
    opp_r,
    plus_r,
    minus_r,
    local_sem,
    send_sem,
    recv_sem,
):
    rows, width = taps.shape
    group = width // blocks
    span = out.shape[1]
    half = span // 2
    c = lax.axis_index("ctx")
    h = lax.axis_index("ch")
    x, core = h // 2, lax.rem(h, 2)
    xs = lax.axis_size("ch") // 2
    partner = x * 2 + 1 - core
    up = lax.rem(x + 1, xs) * 2 + core
    down = lax.rem(x + xs - 1, xs) * 2 + core
    after = lax.rem(c + 1, blocks)

    def local(src, dst, i):
        return pltpu.make_async_copy(src, dst, local_sem.at[i])

    loads = [
        local(taps, tapv, 0),
        local(feat, featv, 1),
        local(split, splitv, 2),
        local(join, joinv, 3),
        local(twist, twistv, 4),
        local(inner, innerv, 5),
        local(decay_in, decay, 10),
        local(short_in, short_w, 11),
        local(skip_in, skip, 12),
    ]
    for load in loads:
        load.start()

    barrier = pltpu.get_barrier_semaphore()

    def greet(off, carry):
        pl.semaphore_signal(
            barrier, inc=1, device_id={"ctx": lax.rem(c + off, blocks)}, device_id_type=MESH
        )
        return carry

    lax.fori_loop(1, blocks, greet, 0)
    for peer in (partner, up, down):
        pl.semaphore_signal(barrier, inc=1, device_id={"ch": peer}, device_id_type=MESH)

    loads[0].wait()
    loads[6].wait()
    places = (c * rows + lax.broadcasted_iota(jnp.int32, (rows, 128), 0)).astype(F32)

    def window(i, carry):
        cols = pl.ds(pl.multiple_of(i * 128, 128), 128)
        rate = decay[:, cols]
        block = tapv[:, cols].astype(F32) * jnp.exp(-rate * places) * jnp.sqrt(2.0 * rate)
        tsend[cols, :] = block.T.astype(BF16)
        return carry

    lax.fori_loop(0, width // 128, window, 0)
    trecv[pl.ds(c * group, group), :] = tsend[pl.ds(c * group, group), :]

    for i in (1, 7, 8):
        loads[i].wait()
    row = lax.broadcasted_iota(jnp.int32, (rows, 128), 0)
    lane = lax.broadcasted_iota(jnp.int32, (rows, 128), 1)
    eight = lax.broadcasted_iota(jnp.int32, (8, 128), 0)
    per_kind = jnp.where(lax.shift_right_logical(lane, 4) == row, 1.0, 0.0).astype(BF16)
    same_channel = lax.rem(lane, group) == lax.rem(row, group)
    per_peer = jnp.where(
        lax.shift_right_logical(lax.broadcasted_iota(jnp.int32, (8, 128), 1), 4) == eight, 1.0, 0.0
    ).astype(BF16)

    def blend(g, cols, rim):
        now = featv[g, :, cols].astype(F32)
        one = jnp.where(row == 0, rim[7:8], pltpu.roll(now, 1, 0))
        two = pltpu.roll(now, 2, 0)
        two = jnp.where(row == 0, rim[6:7], jnp.where(row == 1, rim[7:8], two))
        w = short_w[g, :, cols]
        return w[0:1] * now + w[1:2] * one + w[2:3] * two

    def early(i, carry):
        cols = pl.ds(pl.multiple_of(i * 128, 128), 128)
        nothing = jnp.zeros((8, 128), F32)
        product = blend(1, cols, nothing) * blend(2, cols, nothing)
        psend[cols, :] = product.T.astype(BF16)
        edges = nothing
        for n, g in enumerate((1, 2)):
            head = featv[g, 0:8, cols].astype(F32)
            tail = featv[g, rows - 8 : rows, cols].astype(F32)
            w = short_w[g, :, cols]
            kinds = (
                (2 * n, w[0:1] * head[0:1]),
                (2 * n + 1, w[0:1] * head[1:2] + w[1:2] * head[0:1]),
                (2 * n + 4, w[1:2] * tail[7:8] + w[2:3] * tail[6:7]),
                (2 * n + 5, w[2:3] * tail[7:8]),
            )
            for at, value in kinds:
                edges = jnp.where(eight == at, value, edges)
        turned = jnp.concatenate([edges, jnp.zeros((rows - 8, 128), F32)], axis=0).T
        high, low = halves(turned)
        wide = jnp.where(same_channel, dot(high, per_kind) + dot(low, per_kind), 0.0)
        high, low = halves(wide)
        esend[pl.ds(pl.multiple_of(i * 8, 8), 8), :] = dot(per_peer, high) + dot(per_peer, low)
        return carry

    lax.fori_loop(0, width // 128, early, 0)
    precv[pl.ds(c * group, group), :] = psend[pl.ds(c * group, group), :]
    erecv[pl.ds(c, 1), :] = esend[pl.ds(c, 1), :]

    pl.semaphore_wait(barrier, blocks - 1 + 3)

    def remote(src, dst, i, peer):
        return pltpu.make_async_remote_copy(
            src_ref=src,
            dst_ref=dst,
            send_sem=send_sem.at[i],
            recv_sem=recv_sem.at[i],
            device_id=peer,
            device_id_type=MESH,
        )

    edge = remote(feat.at[:, pl.ds(rows - 8, 8), :], halo, 0, {"ctx": after})
    edge.start()

    def zigzag(i, size):
        return size // 2 + lax.rem(i + 1, 2) * (i // 2) - lax.rem(i, 2) * ((i + 1) // 2)

    def toward(i, j):
        depth_z = blocks // DEPTH_Y
        y = lax.rem(c // depth_z + zigzag(i, DEPTH_Y), DEPTH_Y)
        z = lax.rem(c + zigzag(j, depth_z), depth_z)
        return y * depth_z + z

    depth_z = blocks // DEPTH_Y
    my_y, my_z = c // depth_z, lax.rem(c, depth_z)

    def spread(streams):
        def send(step, z):
            peer = lax.rem(my_y + 2 + step, DEPTH_Y) * depth_z + z
            for src, dst, tall, i in streams:
                remote(
                    src.at[pl.ds(peer * tall, tall), :],
                    dst.at[pl.ds(c * tall, tall), :],
                    i,
                    {"ctx": peer},
                ).start()
            return z

        for far in (4, 3, 5, 2, 6, 1, 7):
            lax.fori_loop(0, DEPTH_Y, send, lax.rem(my_z + far, depth_z))
        for step in (0, 1, 3):
            send(step, my_z)

    def spread_all(src, dst, tall, i):
        count = (blocks - 1) * tall
        return remote(src.at[pl.ds(0, count), :], dst.at[pl.ds(0, count), :], i, {"ctx": after})

    products = (psend, precv, group, 2)
    rims = (esend, erecv, 1, 15)
    filters = (tsend, trecv, group, 1)
    outcomes = (csend, crecv, group, 7)
    spread((rims, products))
    spread((filters,))

    for d in range(xs):
        here = pl.ds(pl.multiple_of((2 * d + core) * span, 128), span)
        there = pl.ds(pl.multiple_of((2 * d + 1 - core) * span, 128), span)
        local(weight.at[:, here], wown.at[:, d * span : (d + 1) * span], 6 + d).start()
        remote(
            weight.at[:, there], wprt.at[:, d * span : (d + 1) * span], 3 + d, {"ch": partner}
        ).start()

    edge.wait()

    def featurize(i, carry):
        cols = pl.ds(pl.multiple_of(i * 128, 128), 128)

        def stream(g):
            return blend(g, cols, jnp.where(c > 0, halo[g, :, cols].astype(F32), 0.0))

        prodv[:, cols] = (stream(1) * stream(2)).astype(BF16)
        first[:, cols] = stream(0)
        return carry

    lax.fori_loop(0, width // 128, featurize, 0)
    for i in range(2, 6):
        loads[i].wait()
    cosine, sine = twistv[0], twistv[1]
    lump = 16
    tall = lump * blocks

    def fine(value, i):
        return dot(value.astype(BF16), innerv[i])

    def lanes(q):
        return slice(q * rows, (q + 1) * rows)

    def tile(q):
        return slice(q * blocks, (q + 1) * blocks)

    def transformed(first_channel):
        data = jnp.concatenate(
            [staged[pl.ds(first_channel + q, blocks, stride=group), :] for q in range(lump)], axis=1
        ).astype(BF16)
        coarse = dot(splitv[...], jnp.concatenate([data, data], axis=0))
        real, imag = coarse[:blocks], coarse[blocks:]
        turned = []
        for q in range(lump):
            r, i = real[:, lanes(q)], imag[:, lanes(q)]
            turned.append(
                jnp.concatenate([r * cosine - i * sine, r * sine + i * cosine], axis=1)
            )
        return fine(jnp.concatenate(turned, axis=0), 0)

    spread_all(*rims).wait_recv()
    spread_all(*products).wait_recv()
    staged[...] = precv[...].astype(F32)
    block_row = lax.broadcasted_iota(jnp.int32, (blocks, 128), 0)
    block_lane = lax.broadcasted_iota(jnp.int32, (blocks, 128), 1)
    rim = erecv[...]
    before = jnp.where(block_row == 0, 0.0, pltpu.roll(rim, 1, 0))
    rim = rim + pltpu.roll(before, 64, 1)
    rim = (rim * pltpu.roll(rim, 96, 1)).astype(BF16).astype(F32)
    for q in range(group):
        at = pl.ds(q, blocks, stride=group)
        zero = pltpu.roll(rim, (128 - q) % 128, 1)
        one = pltpu.roll(rim, 113 - q, 1)
        staged[at, :] = jnp.where(
            block_lane == 0, zero, jnp.where(block_lane == 1, one, staged[at, :])
        )

    def product_spectrum(n, carry):
        spec[pl.ds(pl.multiple_of(n * tall, tall), tall), :] = transformed(n * lump)
        return carry

    lax.fori_loop(0, group // lump, product_spectrum, 0)

    spread_all(*filters).wait_recv()
    staged[...] = trecv[...].astype(F32)

    def through(n, carry):
        data = transformed(n * lump)
        filt = spec[pl.ds(pl.multiple_of(n * tall, tall), tall), :]
        dr, di, fr, fi = data[:, :rows], data[:, rows:], filt[:, :rows], filt[:, rows:]
        back = fine(jnp.concatenate([dr * fr - di * fi, dr * fi + di * fr], axis=1), 1)
        turned = []
        for q in range(lump):
            r, i = back[tile(q), :rows], back[tile(q), rows:]
            turned.append(jnp.concatenate([r * cosine + i * sine, i * cosine - r * sine], axis=0))
        spectrum = jnp.concatenate(turned, axis=1).astype(BF16)
        value = dot(joinv[...], jnp.concatenate([spectrum, spectrum], axis=0))
        for q in range(lump):
            staged[pl.ds(n * lump + q, blocks, stride=group), :] = value[:, lanes(q)]
        return carry

    lax.fori_loop(0, group // lump, through, 0)
    csend[...] = staged[...].astype(BF16)
    spread((outcomes,))
    crecv[pl.ds(c * group, group), :] = csend[pl.ds(c * group, group), :]
    spread_all(*outcomes).wait_recv()

    shares = []
    for i in range(width // 128):
        cols = slice(i * 128, (i + 1) * 128)
        convolved = crecv[cols, :].astype(F32).T
        direct = skip[:, cols] * prodv[:, cols].astype(F32)
        gatedv[:, cols] = (first[:, cols] * (convolved + direct)).astype(BF16)
        share = remote(gatedv.at[:, cols], gatedp.at[:, cols], 16 + i, {"ch": partner})
        share.start()
        shares.append(share)

    for d in range(xs):
        local(weight.at[:, pl.ds(0, span)], wown.at[:, d * span : (d + 1) * span], 6 + d).wait()

    far, high, low = lax.rem(x + 2, xs), lax.rem(x + 1, xs), lax.rem(x + xs - 1, xs)

    def at_side(dest, side):
        return pl.ds(pl.multiple_of(dest * span + side * half, half), half)

    for side in range(2):
        kept[side] = dot(gatedv[...], wown[:, at_side(far, side)])
    for d in range(xs):
        remote(
            weight.at[:, pl.ds(0, span)],
            wprt.at[:, d * span : (d + 1) * span],
            3 + d,
            {"ch": partner},
        ).wait_recv()

    def block(dest, side):
        cols = at_side(dest, side)
        return dot(gatedv[...], wown[:, cols]) + dot(gatedp[...], wprt[:, cols])

    for share in shares:
        share.wait_recv()
    def moved(src, dst, side, piece, i, peer):
        cols = pl.ds(piece * (half // 2), half // 2)
        copy = remote(src.at[side, :, cols], dst.at[side, :, cols], i, {"ch": peer})
        copy.start()
        return copy

    quarter = half // 2
    across = [[], []]
    for piece in range(2):
        for side, peer in ((0, up), (1, down)):
            cols = slice(piece * quarter, (piece + 1) * quarter)
            at = pl.ds(pl.multiple_of(far * span + side * half + piece * quarter, quarter), quarter)
            opp_s[side, :, cols] = (kept[side, :, cols] + dot(gatedp[...], wprt[:, at])).astype(BF16)
            across[side].append(
                moved(opp_s, opp_r, side, piece, 20 + 2 * side + piece, peer)
            )
    plus_s[1] = block(high, 1).astype(BF16)
    plus_one = remote(plus_s.at[1], plus_r.at[1], 11, {"ch": up})
    plus_one.start()
    minus_s[0] = block(low, 0).astype(BF16)
    minus_zero = remote(minus_s.at[0], minus_r.at[0], 12, {"ch": down})
    minus_zero.start()
    kept[0] = block(high, 0)
    kept[1] = block(low, 1)
    added = [[], []]
    for piece in range(2):
        cols = slice(piece * quarter, (piece + 1) * quarter)
        for side, src, dst, peer in ((0, plus_s, plus_r, up), (1, minus_s, minus_r, down)):
            across[side][piece].wait_recv()
            src[side, :, cols] = (
                kept[side, :, cols] + opp_r[side, :, cols].astype(F32)
            ).astype(BF16)
            added[side].append(moved(src, dst, side, piece, 24 + 2 * side + piece, peer))
    kept[0] = block(x, 0)
    kept[1] = block(x, 1)
    minus_zero.wait_recv()
    plus_one.wait_recv()
    kept[0] += minus_r[0].astype(F32)
    kept[1] += plus_r[1].astype(F32)
    for piece in range(2):
        cols = slice(piece * quarter, (piece + 1) * quarter)
        for side, dst in ((0, plus_r), (1, minus_r)):
            added[side][piece].wait_recv()
            out[:, side * half + piece * quarter : side * half + (piece + 1) * quarter] = (
                kept[side, :, cols] + dst[side, :, cols].astype(F32)
            ).astype(BF16)

    for stream in (rims, products, filters, outcomes):
        spread_all(*stream).wait_send()
    for d in range(xs):
        remote(
            weight.at[:, pl.ds(0, span)],
            wprt.at[:, d * span : (d + 1) * span],
            3 + d,
            {"ch": partner},
        ).wait_send()
    for copy in (*shares, *across[0], *across[1], plus_one, minus_zero, *added[0], *added[1]):
        copy.wait_send()


def on_device(features, short_weight, filter_taps, decay_rate, skip_gain, out_weight):
    blocks = lax.axis_size("ctx")
    rows, width = filter_taps.shape
    columns = out_weight.shape[1]
    span = columns // lax.axis_size("ch")
    group = width // blocks
    tables = spectral_tables(blocks, rows)
    stay = lambda value: pltpu.with_memory_space_constraint(value, pltpu.HBM)
    vmem = lambda shape, dtype: pltpu.VMEM(shape, dtype)
    hbm, whole = pl.BlockSpec(memory_space=pltpu.HBM), pl.BlockSpec(memory_space=pltpu.VMEM)

    return pl.pallas_call(
        functools.partial(kernel, blocks),
        out_shape=jax.ShapeDtypeStruct((rows, span), BF16),
        in_specs=[hbm] * 10,
        out_specs=whole,
        scratch_shapes=[
            vmem(features.shape, BF16),
            vmem(filter_taps.shape, BF16),
            vmem(short_weight.shape, F32),
            vmem((1, width), F32),
            vmem((1, width), F32),
            *[vmem(t.shape, t.dtype) for t in tables],
            vmem((3, 8, width), BF16),
            vmem((blocks, 128), F32),
            vmem((blocks, 128), F32),
            *[vmem((width, rows), BF16) for _ in range(6)],
            vmem((rows, width), BF16),
            vmem((rows, width), BF16),
            vmem((width, columns // 2), BF16),
            vmem((width, columns // 2), BF16),
            vmem((rows, width), F32),
            vmem((rows, width), BF16),
            vmem((width, rows), F32),
            vmem((width, 2 * rows), F32),
            vmem((2, rows, span // 2), F32),
            *[vmem((2, rows, span // 2), BF16) for _ in range(6)],
            pltpu.SemaphoreType.DMA((13,)),
            pltpu.SemaphoreType.DMA((28,)),
            pltpu.SemaphoreType.DMA((28,)),
        ],
        compiler_params=pltpu.CompilerParams(
            collective_id=0, has_side_effects=True, vmem_limit_bytes=40000000
        ),
    )(
        stay(features),
        stay(short_weight),
        stay(filter_taps),
        stay(decay_rate[None, :]),
        stay(skip_gain[None, :]),
        stay(out_weight),
        *map(stay, tables),
    )


def solution(mesh):
    return jax.shard_map(
        on_device,
        mesh=mesh,
        in_specs=(
            P(None, "ctx", "ch"),
            P(None, None, "ch"),
            P("ctx", "ch"),
            P("ch"),
            P("ch"),
            P("ch", None),
        ),
        out_specs=P("ctx", "ch"),
        check_vma=False,
    )
```

```python
import functools

import jax
import jax.numpy as jnp
import numpy as np
from jax import lax
from jax.experimental import pallas as pl
from jax.experimental.pallas import tpu as pltpu
from jax.sharding import PartitionSpec as P

MESH = pl.DeviceIdType.MESH
F32, BF16 = jnp.float32, jnp.bfloat16
DEPTH_Y = 4


def spectral_tables(blocks, length):
    total = blocks * length
    coarse = np.arange(blocks)
    fine = np.arange(length)
    stage = np.exp(2j * np.pi * np.outer(coarse + 0.25, coarse) / blocks)
    twist = np.exp(2j * np.pi * np.outer(coarse + 0.25, fine) / total)
    inner = np.exp(2j * np.pi * np.outer(fine, fine) / length)
    down = np.concatenate([stage.real, stage.imag], 0)
    across = np.concatenate([stage.real.T, stage.imag.T], 1)
    forward = np.block([[inner.real, inner.imag], [-inner.imag, inner.real]])
    back = np.conj(inner).T / total
    inverse = np.block([[back.real, back.imag], [-back.imag, back.real]])

    def parts(value):
        value = np.asarray(value, np.float32)
        high = value.astype(jnp.bfloat16)
        return high, (value - high.astype(np.float32)).astype(jnp.bfloat16)

    return (
        jnp.asarray(np.concatenate(parts(down), 1)),
        jnp.asarray(np.concatenate(parts(across), 1)),
        jnp.asarray(np.stack([twist.real, twist.imag]).astype(np.float32)),
        jnp.asarray(np.stack([parts(forward)[0], parts(inverse)[0]])),
    )


def dot(a, b):
    return jnp.dot(a, b, preferred_element_type=F32)


def halves(value):
    high = value.astype(BF16)
    return high, (value - high.astype(F32)).astype(BF16)


def kernel(
    blocks,
    feat,
    short_in,
    taps,
    decay_in,
    skip_in,
    weight,
    split,
    join,
    twist,
    inner,
    out,
    featv,
    tapv,
    short_w,
    decay,
    skip,
    splitv,
    joinv,
    twistv,
    innerv,
    halo,
    esend,
    erecv,
    tsend,
    trecv,
    psend,
    precv,
    csend,
    crecv,
    gatedv,
    gatedp,
    wown,
    wprt,
    first,
    prodv,
    staged,
    spec,
    kept,
    opp_s,
    plus_s,
    minus_s,
    opp_r,
    plus_r,
    minus_r,
    local_sem,
    send_sem,
    recv_sem,
):
    rows, width = taps.shape
    group = width // blocks
    span = out.shape[1]
    half = span // 2
    c = lax.axis_index("ctx")
    h = lax.axis_index("ch")
    x, core = h // 2, lax.rem(h, 2)
    xs = lax.axis_size("ch") // 2
    partner = x * 2 + 1 - core
    up = lax.rem(x + 1, xs) * 2 + core
    down = lax.rem(x + xs - 1, xs) * 2 + core
    after = lax.rem(c + 1, blocks)

    def local(src, dst, i):
        return pltpu.make_async_copy(src, dst, local_sem.at[i])

    loads = [
        local(taps, tapv, 0),
        local(feat, featv, 1),
        local(split, splitv, 2),
        local(join, joinv, 3),
        local(twist, twistv, 4),
        local(inner, innerv, 5),
        local(decay_in, decay, 10),
        local(short_in, short_w, 11),
        local(skip_in, skip, 12),
    ]
    for i in (1, 7, 0, 6, 8, 2, 3, 4, 5):
        loads[i].start()

    barrier = pltpu.get_barrier_semaphore()

    def greet(off, carry):
        pl.semaphore_signal(
            barrier, inc=1, device_id={"ctx": lax.rem(c + off, blocks)}, device_id_type=MESH
        )
        return carry

    lax.fori_loop(1, blocks, greet, 0)
    for peer in (partner, up, down):
        pl.semaphore_signal(barrier, inc=1, device_id={"ch": peer}, device_id_type=MESH)

    for i in (1, 7, 8):
        loads[i].wait()
    row = lax.broadcasted_iota(jnp.int32, (rows, 128), 0)
    lane = lax.broadcasted_iota(jnp.int32, (rows, 128), 1)
    eight = lax.broadcasted_iota(jnp.int32, (8, 128), 0)
    per_kind = jnp.where(lax.shift_right_logical(lane, 4) == row, 1.0, 0.0).astype(BF16)
    same_channel = lax.rem(lane, group) == lax.rem(row, group)
    per_peer = jnp.where(
        lax.shift_right_logical(lax.broadcasted_iota(jnp.int32, (8, 128), 1), 4) == eight, 1.0, 0.0
    ).astype(BF16)

    def blend(g, cols, rim):
        now = featv[g, :, cols].astype(F32)
        one = jnp.where(row == 0, rim[7:8], pltpu.roll(now, 1, 0))
        two = pltpu.roll(now, 2, 0)
        two = jnp.where(row == 0, rim[6:7], jnp.where(row == 1, rim[7:8], two))
        w = short_w[g, :, cols]
        return w[0:1] * now + w[1:2] * one + w[2:3] * two

    def early(i, carry):
        cols = pl.ds(pl.multiple_of(i * 128, 128), 128)
        nothing = jnp.zeros((8, 128), F32)
        product = blend(1, cols, nothing) * blend(2, cols, nothing)
        psend[cols, :] = product.T.astype(BF16)
        edges = nothing
        for n, g in enumerate((1, 2)):
            head = featv[g, 0:8, cols].astype(F32)
            tail = featv[g, rows - 8 : rows, cols].astype(F32)
            w = short_w[g, :, cols]
            kinds = (
                (2 * n, w[0:1] * head[0:1]),
                (2 * n + 1, w[0:1] * head[1:2] + w[1:2] * head[0:1]),
                (2 * n + 4, w[1:2] * tail[7:8] + w[2:3] * tail[6:7]),
                (2 * n + 5, w[2:3] * tail[7:8]),
            )
            for at, value in kinds:
                edges = jnp.where(eight == at, value, edges)
        turned = jnp.concatenate([edges, jnp.zeros((rows - 8, 128), F32)], axis=0).T
        high, low = halves(turned)
        wide = jnp.where(same_channel, dot(high, per_kind) + dot(low, per_kind), 0.0)
        high, low = halves(wide)
        esend[pl.ds(pl.multiple_of(i * 8, 8), 8), :] = dot(per_peer, high) + dot(per_peer, low)
        return carry

    lax.fori_loop(0, width // 128, early, 0)
    precv[pl.ds(c * group, group), :] = psend[pl.ds(c * group, group), :]
    erecv[pl.ds(c, 1), :] = esend[pl.ds(c, 1), :]

    pl.semaphore_wait(barrier, blocks - 1 + 3)

    def remote(src, dst, i, peer):
        return pltpu.make_async_remote_copy(
            src_ref=src,
            dst_ref=dst,
            send_sem=send_sem.at[i],
            recv_sem=recv_sem.at[i],
            device_id=peer,
            device_id_type=MESH,
        )

    edge = remote(feat.at[:, pl.ds(rows - 8, 8), :], halo, 0, {"ctx": after})

    def zigzag(i, size):
        return size // 2 + lax.rem(i + 1, 2) * (i // 2) - lax.rem(i, 2) * ((i + 1) // 2)

    def toward(i, j):
        depth_z = blocks // DEPTH_Y
        y = lax.rem(c // depth_z + zigzag(i, DEPTH_Y), DEPTH_Y)
        z = lax.rem(c + zigzag(j, depth_z), depth_z)
        return y * depth_z + z

    depth_z = blocks // DEPTH_Y
    my_y, my_z = c // depth_z, lax.rem(c, depth_z)

    def spread(streams):
        def send(step, z):
            peer = lax.rem(my_y + 2 + step, DEPTH_Y) * depth_z + z
            for src, dst, tall, i in streams:
                remote(
                    src.at[pl.ds(peer * tall, tall), :],
                    dst.at[pl.ds(c * tall, tall), :],
                    i,
                    {"ctx": peer},
                ).start()
            return z

        for far in (4, 3, 5, 2, 6, 1, 7):
            lax.fori_loop(0, DEPTH_Y, send, lax.rem(my_z + far, depth_z))
        for step in (0, 1, 3):
            send(step, my_z)

    def spread_all(src, dst, tall, i):
        count = (blocks - 1) * tall
        return remote(src.at[pl.ds(0, count), :], dst.at[pl.ds(0, count), :], i, {"ctx": after})

    products = (psend, precv, group, 2)
    rims = (esend, erecv, 1, 15)
    filters = (tsend, trecv, group, 1)
    outcomes = (csend, crecv, group, 7)
    spread((rims, products))
    loads[0].wait()
    loads[6].wait()
    places = (c * rows + lax.broadcasted_iota(jnp.int32, (rows, 128), 0)).astype(F32)

    def window(i, carry):
        cols = pl.ds(pl.multiple_of(i * 128, 128), 128)
        rate = decay[:, cols]
        block = tapv[:, cols].astype(F32) * jnp.exp(-rate * places) * jnp.sqrt(2.0 * rate)
        tsend[cols, :] = block.T.astype(BF16)
        return carry

    lax.fori_loop(0, width // 128, window, 0)
    trecv[pl.ds(c * group, group), :] = tsend[pl.ds(c * group, group), :]

    spread((filters,))

    edge.start()
    edge.wait()

    def featurize(i, carry):
        cols = pl.ds(pl.multiple_of(i * 128, 128), 128)

        def stream(g):
            return blend(g, cols, jnp.where(c > 0, halo[g, :, cols].astype(F32), 0.0))

        prodv[:, cols] = (stream(1) * stream(2)).astype(BF16)
        first[:, cols] = stream(0)
        return carry

    lax.fori_loop(0, width // 128, featurize, 0)
    for i in range(2, 6):
        loads[i].wait()
    cosine, sine = twistv[0], twistv[1]
    lump = 16
    tall = lump * blocks

    def fine(value, i):
        return dot(value.astype(BF16), innerv[i])

    def lanes(q):
        return slice(q * rows, (q + 1) * rows)

    def tile(q):
        return slice(q * blocks, (q + 1) * blocks)

    def transformed(first_channel):
        data = jnp.concatenate(
            [staged[pl.ds(first_channel + q, blocks, stride=group), :] for q in range(lump)], axis=1
        ).astype(BF16)
        coarse = dot(splitv[...], jnp.concatenate([data, data], axis=0))
        real, imag = coarse[:blocks], coarse[blocks:]
        turned = []
        for q in range(lump):
            r, i = real[:, lanes(q)], imag[:, lanes(q)]
            turned.append(
                jnp.concatenate([r * cosine - i * sine, r * sine + i * cosine], axis=1)
            )
        return fine(jnp.concatenate(turned, axis=0), 0)

    spread_all(*rims).wait_recv()
    spread_all(*products).wait_recv()
    for d in range(xs):
        here = pl.ds(pl.multiple_of((2 * d + core) * span, 128), span)
        there = pl.ds(pl.multiple_of((2 * d + 1 - core) * span, 128), span)
        local(weight.at[:, here], wown.at[:, d * span : (d + 1) * span], 6 + d).start()
        remote(
            weight.at[:, there], wprt.at[:, d * span : (d + 1) * span], 3 + d, {"ch": partner}
        ).start()

    staged[...] = precv[...].astype(F32)
    block_row = lax.broadcasted_iota(jnp.int32, (blocks, 128), 0)
    block_lane = lax.broadcasted_iota(jnp.int32, (blocks, 128), 1)
    rim = erecv[...]
    before = jnp.where(block_row == 0, 0.0, pltpu.roll(rim, 1, 0))
    rim = rim + pltpu.roll(before, 64, 1)
    rim = (rim * pltpu.roll(rim, 96, 1)).astype(BF16).astype(F32)
    for q in range(group):
        at = pl.ds(q, blocks, stride=group)
        zero = pltpu.roll(rim, (128 - q) % 128, 1)
        one = pltpu.roll(rim, 113 - q, 1)
        staged[at, :] = jnp.where(
            block_lane == 0, zero, jnp.where(block_lane == 1, one, staged[at, :])
        )

    def product_spectrum(n, carry):
        spec[pl.ds(pl.multiple_of(n * tall, tall), tall), :] = transformed(n * lump)
        return carry

    lax.fori_loop(0, group // lump, product_spectrum, 0)

    spread_all(*filters).wait_recv()
    staged[...] = trecv[...].astype(F32)

    def through(n, carry):
        data = transformed(n * lump)
        filt = spec[pl.ds(pl.multiple_of(n * tall, tall), tall), :]
        dr, di, fr, fi = data[:, :rows], data[:, rows:], filt[:, :rows], filt[:, rows:]
        back = fine(jnp.concatenate([dr * fr - di * fi, dr * fi + di * fr], axis=1), 1)
        turned = []
        for q in range(lump):
            r, i = back[tile(q), :rows], back[tile(q), rows:]
            turned.append(jnp.concatenate([r * cosine + i * sine, i * cosine - r * sine], axis=0))
        spectrum = jnp.concatenate(turned, axis=1).astype(BF16)
        value = dot(joinv[...], jnp.concatenate([spectrum, spectrum], axis=0))
        for q in range(lump):
            staged[pl.ds(n * lump + q, blocks, stride=group), :] = value[:, lanes(q)]
        return carry

    lax.fori_loop(0, group // lump, through, 0)
    csend[...] = staged[...].astype(BF16)
    spread((outcomes,))
    crecv[pl.ds(c * group, group), :] = csend[pl.ds(c * group, group), :]
    spread_all(*outcomes).wait_recv()

    shares = []
    for i in range(width // 128):
        cols = slice(i * 128, (i + 1) * 128)
        convolved = crecv[cols, :].astype(F32).T
        direct = skip[:, cols] * prodv[:, cols].astype(F32)
        gatedv[:, cols] = (first[:, cols] * (convolved + direct)).astype(BF16)
        share = remote(gatedv.at[:, cols], gatedp.at[:, cols], 16 + i, {"ch": partner})
        share.start()
        shares.append(share)

    for d in range(xs):
        local(weight.at[:, pl.ds(0, span)], wown.at[:, d * span : (d + 1) * span], 6 + d).wait()

    far, high, low = lax.rem(x + 2, xs), lax.rem(x + 1, xs), lax.rem(x + xs - 1, xs)

    def at_side(dest, side):
        return pl.ds(pl.multiple_of(dest * span + side * half, half), half)

    for side in range(2):
        kept[side] = dot(gatedv[...], wown[:, at_side(far, side)])
    for d in range(xs):
        remote(
            weight.at[:, pl.ds(0, span)],
            wprt.at[:, d * span : (d + 1) * span],
            3 + d,
            {"ch": partner},
        ).wait_recv()

    def block(dest, side):
        cols = at_side(dest, side)
        return dot(gatedv[...], wown[:, cols]) + dot(gatedp[...], wprt[:, cols])

    for share in shares:
        share.wait_recv()
    def moved(src, dst, side, piece, i, peer):
        cols = pl.ds(piece * (half // 2), half // 2)
        copy = remote(src.at[side, :, cols], dst.at[side, :, cols], i, {"ch": peer})
        copy.start()
        return copy

    quarter = half // 2
    across = [[], []]
    for piece in range(2):
        for side, peer in ((0, up), (1, down)):
            cols = slice(piece * quarter, (piece + 1) * quarter)
            at = pl.ds(pl.multiple_of(far * span + side * half + piece * quarter, quarter), quarter)
            opp_s[side, :, cols] = (kept[side, :, cols] + dot(gatedp[...], wprt[:, at])).astype(BF16)
            across[side].append(
                moved(opp_s, opp_r, side, piece, 20 + 2 * side + piece, peer)
            )
    plus_s[1] = block(high, 1).astype(BF16)
    plus_one = remote(plus_s.at[1], plus_r.at[1], 11, {"ch": up})
    plus_one.start()
    minus_s[0] = block(low, 0).astype(BF16)
    minus_zero = remote(minus_s.at[0], minus_r.at[0], 12, {"ch": down})
    minus_zero.start()
    kept[0] = block(high, 0)
    kept[1] = block(low, 1)
    added = [[], []]
    for piece in range(2):
        cols = slice(piece * quarter, (piece + 1) * quarter)
        for side, src, dst, peer in ((0, plus_s, plus_r, up), (1, minus_s, minus_r, down)):
            across[side][piece].wait_recv()
            src[side, :, cols] = (
                kept[side, :, cols] + opp_r[side, :, cols].astype(F32)
            ).astype(BF16)
            added[side].append(moved(src, dst, side, piece, 24 + 2 * side + piece, peer))
    kept[0] = block(x, 0)
    kept[1] = block(x, 1)
    minus_zero.wait_recv()
    plus_one.wait_recv()
    kept[0] += minus_r[0].astype(F32)
    kept[1] += plus_r[1].astype(F32)
    for piece in range(2):
        cols = slice(piece * quarter, (piece + 1) * quarter)
        for side, dst in ((0, plus_r), (1, minus_r)):
            added[side][piece].wait_recv()
            out[:, side * half + piece * quarter : side * half + (piece + 1) * quarter] = (
                kept[side, :, cols] + dst[side, :, cols].astype(F32)
            ).astype(BF16)

    for stream in (rims, products, filters, outcomes):
        spread_all(*stream).wait_send()
    for d in range(xs):
        remote(
            weight.at[:, pl.ds(0, span)],
            wprt.at[:, d * span : (d + 1) * span],
            3 + d,
            {"ch": partner},
        ).wait_send()
    for copy in (*shares, *across[0], *across[1], plus_one, minus_zero, *added[0], *added[1]):
        copy.wait_send()


def on_device(features, short_weight, filter_taps, decay_rate, skip_gain, out_weight):
    blocks = lax.axis_size("ctx")
    rows, width = filter_taps.shape
    columns = out_weight.shape[1]
    span = columns // lax.axis_size("ch")
    group = width // blocks
    tables = spectral_tables(blocks, rows)
    stay = lambda value: pltpu.with_memory_space_constraint(value, pltpu.HBM)
    vmem = lambda shape, dtype: pltpu.VMEM(shape, dtype)
    hbm, whole = pl.BlockSpec(memory_space=pltpu.HBM), pl.BlockSpec(memory_space=pltpu.VMEM)

    return pl.pallas_call(
        functools.partial(kernel, blocks),
        out_shape=jax.ShapeDtypeStruct((rows, span), BF16),
        in_specs=[hbm] * 10,
        out_specs=whole,
        scratch_shapes=[
            vmem(features.shape, BF16),
            vmem(filter_taps.shape, BF16),
            vmem(short_weight.shape, F32),
            vmem((1, width), F32),
            vmem((1, width), F32),
            *[vmem(t.shape, t.dtype) for t in tables],
            vmem((3, 8, width), BF16),
            vmem((blocks, 128), F32),
            vmem((blocks, 128), F32),
            *[vmem((width, rows), BF16) for _ in range(6)],
            vmem((rows, width), BF16),
            vmem((rows, width), BF16),
            vmem((width, columns // 2), BF16),
            vmem((width, columns // 2), BF16),
            vmem((rows, width), F32),
            vmem((rows, width), BF16),
            vmem((width, rows), F32),
            vmem((width, 2 * rows), F32),
            vmem((2, rows, span // 2), F32),
            *[vmem((2, rows, span // 2), BF16) for _ in range(6)],
            pltpu.SemaphoreType.DMA((13,)),
            pltpu.SemaphoreType.DMA((28,)),
            pltpu.SemaphoreType.DMA((28,)),
        ],
        compiler_params=pltpu.CompilerParams(
            collective_id=0, has_side_effects=True, vmem_limit_bytes=40000000
        ),
    )(
        stay(features),
        stay(short_weight),
        stay(filter_taps),
        stay(decay_rate[None, :]),
        stay(skip_gain[None, :]),
        stay(out_weight),
        *map(stay, tables),
    )


def solution(mesh):
    return jax.shard_map(
        on_device,
        mesh=mesh,
        in_specs=(
            P(None, "ctx", "ch"),
            P(None, None, "ch"),
            P("ctx", "ch"),
            P("ch"),
            P("ch"),
            P("ch", None),
        ),
        out_specs=P("ctx", "ch"),
        check_vma=False,
    )
```

```python
import functools

import jax
import jax.numpy as jnp
import numpy as np
from jax import lax
from jax.experimental import pallas as pl
from jax.experimental.pallas import tpu as pltpu
from jax.sharding import PartitionSpec as P

MESH = pl.DeviceIdType.MESH
F32, BF16 = jnp.float32, jnp.bfloat16
DEPTH_Y = 4


def spectral_tables(blocks, length):
    total = blocks * length
    coarse = np.arange(blocks)
    fine = np.arange(length)
    stage = np.exp(2j * np.pi * np.outer(coarse + 0.25, coarse) / blocks)
    twist = np.exp(2j * np.pi * np.outer(coarse + 0.25, fine) / total)
    inner = np.exp(2j * np.pi * np.outer(fine, fine) / length)
    down = np.concatenate([stage.real, stage.imag], 0)
    across = np.concatenate([stage.real.T, stage.imag.T], 1)
    forward = np.block([[inner.real, inner.imag], [-inner.imag, inner.real]])
    back = np.conj(inner).T / total
    inverse = np.block([[back.real, back.imag], [-back.imag, back.real]])

    def parts(value):
        value = np.asarray(value, np.float32)
        high = value.astype(jnp.bfloat16)
        return high, (value - high.astype(np.float32)).astype(jnp.bfloat16)

    return (
        jnp.asarray(np.concatenate(parts(down), 1)),
        jnp.asarray(np.concatenate(parts(across), 1)),
        jnp.asarray(np.stack([twist.real, twist.imag]).astype(np.float32)),
        jnp.asarray(np.stack([parts(forward)[0], parts(inverse)[0]])),
    )


def dot(a, b):
    return jnp.dot(a, b, preferred_element_type=F32)


def halves(value):
    high = value.astype(BF16)
    return high, (value - high.astype(F32)).astype(BF16)


def kernel(
    blocks,
    feat,
    short_in,
    taps,
    decay_in,
    skip_in,
    weight,
    split,
    join,
    twist,
    inner,
    out,
    featv,
    tapv,
    short_w,
    decay,
    skip,
    splitv,
    joinv,
    twistv,
    innerv,
    halo,
    esend,
    erecv,
    tsend,
    trecv,
    psend,
    precv,
    csend,
    crecv,
    gatedv,
    gatedp,
    wown,
    wprt,
    first,
    prodv,
    staged,
    spec,
    kept,
    opp_s,
    plus_s,
    minus_s,
    opp_r,
    plus_r,
    minus_r,
    local_sem,
    send_sem,
    recv_sem,
):
    rows, width = taps.shape
    group = width // blocks
    span = out.shape[1]
    half = span // 2
    c = lax.axis_index("ctx")
    h = lax.axis_index("ch")
    x, core = h // 2, lax.rem(h, 2)
    xs = lax.axis_size("ch") // 2
    partner = x * 2 + 1 - core
    up = lax.rem(x + 1, xs) * 2 + core
    down = lax.rem(x + xs - 1, xs) * 2 + core
    after = lax.rem(c + 1, blocks)

    def local(src, dst, i):
        return pltpu.make_async_copy(src, dst, local_sem.at[i])

    loads = [
        local(taps, tapv, 0),
        local(feat, featv, 1),
        local(split, splitv, 2),
        local(join, joinv, 3),
        local(twist, twistv, 4),
        local(inner, innerv, 5),
        local(decay_in, decay, 10),
        local(short_in, short_w, 11),
        local(skip_in, skip, 12),
    ]
    for i in (1, 7, 0, 6, 8, 2, 3, 4, 5):
        loads[i].start()

    barrier = pltpu.get_barrier_semaphore()

    def greet(off, carry):
        pl.semaphore_signal(
            barrier, inc=1, device_id={"ctx": lax.rem(c + off, blocks)}, device_id_type=MESH
        )
        return carry

    lax.fori_loop(1, blocks, greet, 0)
    for peer in (partner, up, down):
        pl.semaphore_signal(barrier, inc=1, device_id={"ch": peer}, device_id_type=MESH)

    for i in (1, 7, 8):
        loads[i].wait()
    row = lax.broadcasted_iota(jnp.int32, (rows, 128), 0)
    lane = lax.broadcasted_iota(jnp.int32, (rows, 128), 1)
    eight = lax.broadcasted_iota(jnp.int32, (8, 128), 0)
    per_kind = jnp.where(lax.shift_right_logical(lane, 4) == row, 1.0, 0.0).astype(BF16)
    same_channel = lax.rem(lane, group) == lax.rem(row, group)
    per_peer = jnp.where(
        lax.shift_right_logical(lax.broadcasted_iota(jnp.int32, (8, 128), 1), 4) == eight, 1.0, 0.0
    ).astype(BF16)

    def blend(g, cols, rim):
        now = featv[g, :, cols].astype(F32)
        one = jnp.where(row == 0, rim[7:8], pltpu.roll(now, 1, 0))
        two = pltpu.roll(now, 2, 0)
        two = jnp.where(row == 0, rim[6:7], jnp.where(row == 1, rim[7:8], two))
        w = short_w[g, :, cols]
        return w[0:1] * now + w[1:2] * one + w[2:3] * two

    def early(i, carry):
        cols = pl.ds(pl.multiple_of(i * 128, 128), 128)
        nothing = jnp.zeros((8, 128), F32)
        product = blend(1, cols, nothing) * blend(2, cols, nothing)
        psend[cols, :] = product.T.astype(BF16)
        edges = nothing
        for n, g in enumerate((1, 2)):
            head = featv[g, 0:8, cols].astype(F32)
            tail = featv[g, rows - 8 : rows, cols].astype(F32)
            w = short_w[g, :, cols]
            kinds = (
                (2 * n, w[0:1] * head[0:1]),
                (2 * n + 1, w[0:1] * head[1:2] + w[1:2] * head[0:1]),
                (2 * n + 4, w[1:2] * tail[7:8] + w[2:3] * tail[6:7]),
                (2 * n + 5, w[2:3] * tail[7:8]),
            )
            for at, value in kinds:
                edges = jnp.where(eight == at, value, edges)
        turned = jnp.concatenate([edges, jnp.zeros((rows - 8, 128), F32)], axis=0).T
        high, low = halves(turned)
        wide = jnp.where(same_channel, dot(high, per_kind) + dot(low, per_kind), 0.0)
        high, low = halves(wide)
        esend[pl.ds(pl.multiple_of(i * 8, 8), 8), :] = dot(per_peer, high) + dot(per_peer, low)
        return carry

    lax.fori_loop(0, width // 128, early, 0)
    precv[pl.ds(c * group, group), :] = psend[pl.ds(c * group, group), :]
    erecv[pl.ds(c, 1), :] = esend[pl.ds(c, 1), :]

    pl.semaphore_wait(barrier, blocks - 1 + 3)

    def remote(src, dst, i, peer):
        return pltpu.make_async_remote_copy(
            src_ref=src,
            dst_ref=dst,
            send_sem=send_sem.at[i],
            recv_sem=recv_sem.at[i],
            device_id=peer,
            device_id_type=MESH,
        )

    edge = remote(feat.at[:, pl.ds(rows - 8, 8), :], halo, 0, {"ctx": after})

    def zigzag(i, size):
        return size // 2 + lax.rem(i + 1, 2) * (i // 2) - lax.rem(i, 2) * ((i + 1) // 2)

    def toward(i, j):
        depth_z = blocks // DEPTH_Y
        y = lax.rem(c // depth_z + zigzag(i, DEPTH_Y), DEPTH_Y)
        z = lax.rem(c + zigzag(j, depth_z), depth_z)
        return y * depth_z + z

    depth_z = blocks // DEPTH_Y
    my_y, my_z = c // depth_z, lax.rem(c, depth_z)

    def spread(streams):
        def send(step, z):
            peer = lax.rem(my_y + 2 + step, DEPTH_Y) * depth_z + z
            for src, dst, tall, i in streams:
                remote(
                    src.at[pl.ds(peer * tall, tall), :],
                    dst.at[pl.ds(c * tall, tall), :],
                    i,
                    {"ctx": peer},
                ).start()
            return z

        for far in (4, 3, 5, 2, 6, 1, 7):
            lax.fori_loop(0, DEPTH_Y, send, lax.rem(my_z + far, depth_z))
        for step in (0, 1, 3):
            send(step, my_z)

    def spread_all(src, dst, tall, i):
        count = (blocks - 1) * tall
        return remote(src.at[pl.ds(0, count), :], dst.at[pl.ds(0, count), :], i, {"ctx": after})

    products = (psend, precv, group, 2)
    rims = (esend, erecv, 1, 15)
    filters = (tsend, trecv, group, 1)
    outcomes = (csend, crecv, group, 7)
    spread((rims, products))
    loads[0].wait()
    loads[6].wait()
    places = (c * rows + lax.broadcasted_iota(jnp.int32, (rows, 128), 0)).astype(F32)

    def window(i, carry):
        cols = pl.ds(pl.multiple_of(i * 128, 128), 128)
        rate = decay[:, cols]
        block = tapv[:, cols].astype(F32) * jnp.exp(-rate * places) * jnp.sqrt(2.0 * rate)
        tsend[cols, :] = block.T.astype(BF16)
        return carry

    lax.fori_loop(0, width // 128, window, 0)
    trecv[pl.ds(c * group, group), :] = tsend[pl.ds(c * group, group), :]

    spread((filters,))

    for i in range(2, 6):
        loads[i].wait()
    cosine, sine = twistv[0], twistv[1]
    lump = 16
    tall = lump * blocks

    def fine(value, i):
        return dot(value.astype(BF16), innerv[i])

    def lanes(q):
        return slice(q * rows, (q + 1) * rows)

    def tile(q):
        return slice(q * blocks, (q + 1) * blocks)

    def transformed(first_channel):
        data = jnp.concatenate(
            [staged[pl.ds(first_channel + q, blocks, stride=group), :] for q in range(lump)], axis=1
        ).astype(BF16)
        coarse = dot(splitv[...], jnp.concatenate([data, data], axis=0))
        real, imag = coarse[:blocks], coarse[blocks:]
        turned = []
        for q in range(lump):
            r, i = real[:, lanes(q)], imag[:, lanes(q)]
            turned.append(
                jnp.concatenate([r * cosine - i * sine, r * sine + i * cosine], axis=1)
            )
        return fine(jnp.concatenate(turned, axis=0), 0)

    spread_all(*rims).wait_recv()
    spread_all(*products).wait_recv()
    edge.start()
    for d in range(xs):
        here = pl.ds(pl.multiple_of((2 * d + core) * span, 128), span)
        there = pl.ds(pl.multiple_of((2 * d + 1 - core) * span, 128), span)
        local(weight.at[:, here], wown.at[:, d * span : (d + 1) * span], 6 + d).start()
        remote(
            weight.at[:, there], wprt.at[:, d * span : (d + 1) * span], 3 + d, {"ch": partner}
        ).start()

    staged[...] = precv[...].astype(F32)
    block_row = lax.broadcasted_iota(jnp.int32, (blocks, 128), 0)
    block_lane = lax.broadcasted_iota(jnp.int32, (blocks, 128), 1)
    rim = erecv[...]
    before = jnp.where(block_row == 0, 0.0, pltpu.roll(rim, 1, 0))
    rim = rim + pltpu.roll(before, 64, 1)
    rim = (rim * pltpu.roll(rim, 96, 1)).astype(BF16).astype(F32)
    for q in range(group):
        at = pl.ds(q, blocks, stride=group)
        zero = pltpu.roll(rim, (128 - q) % 128, 1)
        one = pltpu.roll(rim, 113 - q, 1)
        staged[at, :] = jnp.where(
            block_lane == 0, zero, jnp.where(block_lane == 1, one, staged[at, :])
        )

    def product_spectrum(n, carry):
        spec[pl.ds(pl.multiple_of(n * tall, tall), tall), :] = transformed(n * lump)
        return carry

    lax.fori_loop(0, group // lump, product_spectrum, 0)

    spread_all(*filters).wait_recv()
    staged[...] = trecv[...].astype(F32)

    def through(n, carry):
        data = transformed(n * lump)
        filt = spec[pl.ds(pl.multiple_of(n * tall, tall), tall), :]
        dr, di, fr, fi = data[:, :rows], data[:, rows:], filt[:, :rows], filt[:, rows:]
        back = fine(jnp.concatenate([dr * fr - di * fi, dr * fi + di * fr], axis=1), 1)
        turned = []
        for q in range(lump):
            r, i = back[tile(q), :rows], back[tile(q), rows:]
            turned.append(jnp.concatenate([r * cosine + i * sine, i * cosine - r * sine], axis=0))
        spectrum = jnp.concatenate(turned, axis=1).astype(BF16)
        value = dot(joinv[...], jnp.concatenate([spectrum, spectrum], axis=0))
        for q in range(lump):
            staged[pl.ds(n * lump + q, blocks, stride=group), :] = value[:, lanes(q)]
        return carry

    lax.fori_loop(0, group // lump, through, 0)
    csend[...] = staged[...].astype(BF16)
    spread((outcomes,))
    edge.wait()

    def featurize(i, carry):
        cols = pl.ds(pl.multiple_of(i * 128, 128), 128)

        def stream(g):
            return blend(g, cols, jnp.where(c > 0, halo[g, :, cols].astype(F32), 0.0))

        prodv[:, cols] = (stream(1) * stream(2)).astype(BF16)
        first[:, cols] = stream(0)
        return carry

    lax.fori_loop(0, width // 128, featurize, 0)
    crecv[pl.ds(c * group, group), :] = csend[pl.ds(c * group, group), :]
    spread_all(*outcomes).wait_recv()

    shares = []
    for i in range(width // 128):
        cols = slice(i * 128, (i + 1) * 128)
        convolved = crecv[cols, :].astype(F32).T
        direct = skip[:, cols] * prodv[:, cols].astype(F32)
        gatedv[:, cols] = (first[:, cols] * (convolved + direct)).astype(BF16)
        share = remote(gatedv.at[:, cols], gatedp.at[:, cols], 16 + i, {"ch": partner})
        share.start()
        shares.append(share)

    for d in range(xs):
        local(weight.at[:, pl.ds(0, span)], wown.at[:, d * span : (d + 1) * span], 6 + d).wait()

    far, high, low = lax.rem(x + 2, xs), lax.rem(x + 1, xs), lax.rem(x + xs - 1, xs)

    def at_side(dest, side):
        return pl.ds(pl.multiple_of(dest * span + side * half, half), half)

    for side in range(2):
        kept[side] = dot(gatedv[...], wown[:, at_side(far, side)])
    for d in range(xs):
        remote(
            weight.at[:, pl.ds(0, span)],
            wprt.at[:, d * span : (d + 1) * span],
            3 + d,
            {"ch": partner},
        ).wait_recv()

    def block(dest, side):
        cols = at_side(dest, side)
        return dot(gatedv[...], wown[:, cols]) + dot(gatedp[...], wprt[:, cols])

    for share in shares:
        share.wait_recv()
    def moved(src, dst, side, piece, i, peer):
        cols = pl.ds(piece * (half // 2), half // 2)
        copy = remote(src.at[side, :, cols], dst.at[side, :, cols], i, {"ch": peer})
        copy.start()
        return copy

    quarter = half // 2
    across = [[], []]
    for piece in range(2):
        for side, peer in ((0, up), (1, down)):
            cols = slice(piece * quarter, (piece + 1) * quarter)
            at = pl.ds(pl.multiple_of(far * span + side * half + piece * quarter, quarter), quarter)
            opp_s[side, :, cols] = (kept[side, :, cols] + dot(gatedp[...], wprt[:, at])).astype(BF16)
            across[side].append(
                moved(opp_s, opp_r, side, piece, 20 + 2 * side + piece, peer)
            )
    plus_s[1] = block(high, 1).astype(BF16)
    plus_one = remote(plus_s.at[1], plus_r.at[1], 11, {"ch": up})
    plus_one.start()
    minus_s[0] = block(low, 0).astype(BF16)
    minus_zero = remote(minus_s.at[0], minus_r.at[0], 12, {"ch": down})
    minus_zero.start()
    kept[0] = block(high, 0)
    kept[1] = block(low, 1)
    added = [[], []]
    for piece in range(2):
        cols = slice(piece * quarter, (piece + 1) * quarter)
        for side, src, dst, peer in ((0, plus_s, plus_r, up), (1, minus_s, minus_r, down)):
            across[side][piece].wait_recv()
            src[side, :, cols] = (
                kept[side, :, cols] + opp_r[side, :, cols].astype(F32)
            ).astype(BF16)
            added[side].append(moved(src, dst, side, piece, 24 + 2 * side + piece, peer))
    kept[0] = block(x, 0)
    kept[1] = block(x, 1)
    minus_zero.wait_recv()
    plus_one.wait_recv()
    kept[0] += minus_r[0].astype(F32)
    kept[1] += plus_r[1].astype(F32)
    for piece in range(2):
        cols = slice(piece * quarter, (piece + 1) * quarter)
        for side, dst in ((0, plus_r), (1, minus_r)):
            added[side][piece].wait_recv()
            out[:, side * half + piece * quarter : side * half + (piece + 1) * quarter] = (
                kept[side, :, cols] + dst[side, :, cols].astype(F32)
            ).astype(BF16)

    for stream in (rims, products, filters, outcomes):
        spread_all(*stream).wait_send()
    for d in range(xs):
        remote(
            weight.at[:, pl.ds(0, span)],
            wprt.at[:, d * span : (d + 1) * span],
            3 + d,
            {"ch": partner},
        ).wait_send()
    for copy in (*shares, *across[0], *across[1], plus_one, minus_zero, *added[0], *added[1]):
        copy.wait_send()


def on_device(features, short_weight, filter_taps, decay_rate, skip_gain, out_weight):
    blocks = lax.axis_size("ctx")
    rows, width = filter_taps.shape
    columns = out_weight.shape[1]
    span = columns // lax.axis_size("ch")
    group = width // blocks
    tables = spectral_tables(blocks, rows)
    stay = lambda value: pltpu.with_memory_space_constraint(value, pltpu.HBM)
    vmem = lambda shape, dtype: pltpu.VMEM(shape, dtype)
    hbm, whole = pl.BlockSpec(memory_space=pltpu.HBM), pl.BlockSpec(memory_space=pltpu.VMEM)

    return pl.pallas_call(
        functools.partial(kernel, blocks),
        out_shape=jax.ShapeDtypeStruct((rows, span), BF16),
        in_specs=[hbm] * 10,
        out_specs=whole,
        scratch_shapes=[
            vmem(features.shape, BF16),
            vmem(filter_taps.shape, BF16),
            vmem(short_weight.shape, F32),
            vmem((1, width), F32),
            vmem((1, width), F32),
            *[vmem(t.shape, t.dtype) for t in tables],
            vmem((3, 8, width), BF16),
            vmem((blocks, 128), F32),
            vmem((blocks, 128), F32),
            *[vmem((width, rows), BF16) for _ in range(6)],
            vmem((rows, width), BF16),
            vmem((rows, width), BF16),
            vmem((width, columns // 2), BF16),
            vmem((width, columns // 2), BF16),
            vmem((rows, width), F32),
            vmem((rows, width), BF16),
            vmem((width, rows), F32),
            vmem((width, 2 * rows), F32),
            vmem((2, rows, span // 2), F32),
            *[vmem((2, rows, span // 2), BF16) for _ in range(6)],
            pltpu.SemaphoreType.DMA((13,)),
            pltpu.SemaphoreType.DMA((28,)),
            pltpu.SemaphoreType.DMA((28,)),
        ],
        compiler_params=pltpu.CompilerParams(
            collective_id=0, has_side_effects=True, vmem_limit_bytes=40000000
        ),
    )(
        stay(features),
        stay(short_weight),
        stay(filter_taps),
        stay(decay_rate[None, :]),
        stay(skip_gain[None, :]),
        stay(out_weight),
        *map(stay, tables),
    )


def solution(mesh):
    return jax.shard_map(
        on_device,
        mesh=mesh,
        in_specs=(
            P(None, "ctx", "ch"),
            P(None, None, "ch"),
            P("ctx", "ch"),
            P("ch"),
            P("ch"),
            P("ch", None),
        ),
        out_specs=P("ctx", "ch"),
        check_vma=False,
    )
```
